256 devices in a mesh: rep: 32 (over x, z), tp: 8 (over y, core).
Axes of the slice: x: 4, y: 4, z: 8, core: 2. Of those that a mesh axis runs over, the one named last changes fastest.
Arguments:
- hidden: bfloat16 [256, 2, 8192], P('rep'), may hold values from -6 to 6
- queries: bfloat16 [256, 2, 8192], P('rep', None, 'tp')
- key_weight: bfloat16 [8192, 1024], P(None, 'tp'), may hold values from -0.0625 to 0.0625
- value_weight: bfloat16 [8192, 1024], P(None, 'tp'), may hold values from -0.0625 to 0.0625
- adapter_down_weight: bfloat16 [512, 8192, 64], P('rep', 'tp'), may hold values from -0.0625 to 0.0625
- adapter_up_weight: bfloat16 [512, 64, 1024], P('rep', None, 'tp'), may hold values from -0.75 to 0.75
- row_adapter_index: int32 [256], P('rep'), may hold values from 0 to 511, as said below
- adapter_home_slot: int32 [512], replicated, may hold values from 0 to 511, as said below
- row_page_table: int32 [256, 8], P('rep'), may hold values from 0 to 63, as said below
- lengths: int32 [32, 8], P('rep'), may hold values from 1 to 1024, 5120 in all within a row
- row_serving_slot: int32 [256], P('rep'), may hold values from 0 to 511, as said below
- paged_key_cache: bfloat16 [2048, 128, 1024], P('rep', None, 'tp'), may hold values from -6 to 6
- paged_value_cache: bfloat16 [2048, 128, 1024], P('rep', None, 'tp'), may hold values from -6 to 6
Outputs:
- attended: bfloat16 [512, 2, 8192], P('rep', None, 'tp')
The draws below stay inside these ranges and needn't reach their ends.
Inputs may be any that keep to these rules, and one draw needn't show every extreme that they name: `row_adapter_index`: adapter a's maps are adapter_down_weight[adapter_home_slot[a]] and adapter_up_weight[adapter_home_slot[a]]; the rows of one replica use adapters with distinct home slots // 16. `adapter_home_slot`: A permutation. `row_page_table`: the rows of one replica use distinct pages of its pool. `lengths`: each sequence holds at most 1024 positions; the 8 sequences of one replica (one line of the array) together hold 5120 positions. `row_serving_slot`: slots are distinct. A quarter of the replicas are preempted: their rows name slots 8 to 15 of other replicas, at most 2 rows of one replica in one other replica; every other replica keeps row i of its own in its slot i.
All inputs are finite; a program needn't handle non-finite values.
Results may differ from the reference program's by a relative error of at most 0.0051.
Values may be sent and summed in bfloat16 or wider, within the bound.
A program may use at most 64 MiB of HBM per device.

```python
import math
import jax
import jax.numpy as jnp
import numpy as np
from jax import lax

MODEL_WIDTH = 8192
HEADS = 64
KEY_VALUE_HEADS = 8
HEAD_SIZE = 128
ADAPTER_RANK = 64
ADP_DEV = 16
ROWS = 8
PAGE = 128
PAGES_ROW = 8
ADAPTER_TOTAL = 512
POOL = 64
MAXLEN = 1024
SLOTS = 16
N_REP = 32


def adapter_parts(key):
    home_slot = jax.random.permutation(jax.random.fold_in(key, 7), ADAPTER_TOTAL)
    inverse = jnp.argsort(home_slot)
    keys = jax.random.split(jax.random.fold_in(key, 11), N_REP)
    owners = jax.vmap(lambda single: jax.random.permutation(single, N_REP)[:ROWS])(keys)
    within = jax.random.randint(jax.random.fold_in(key, 13), (N_REP, ROWS), 0, ADP_DEV)
    chosen = inverse[owners * ADP_DEV + within].reshape(-1)
    return (home_slot.astype(jnp.int32), chosen.astype(jnp.int32))


def draw_adapter_home_slot(key, part):
    return adapter_parts(key)[0]


def draw_row_adapter_index(key, part):
    return adapter_parts(key)[1]


def pool_tables(key):
    keys = jax.random.split(jax.random.fold_in(key, 17), N_REP)
    return jax.vmap(lambda single: jax.random.permutation(single, POOL))(keys)


def draw_row_page_table(key, part):
    return pool_tables(key).reshape(N_REP * ROWS, PAGES_ROW).astype(jnp.int32)


def cache_page(key, page):
    single = jax.random.fold_in(jax.random.fold_in(key, 23), page)
    return jnp.clip(jax.random.normal(single, (PAGE, KEY_VALUE_HEADS * HEAD_SIZE), jnp.float32), -6.0, 6.0)


def draw_paged_key_cache(key, part):
    pages = jnp.arange(N_REP * POOL, dtype=jnp.int32)
    keys = jax.vmap(lambda page: cache_page(key, page))(pages)
    return keys.astype(jnp.bfloat16)


def draw_row_serving_slot(key, part):
    quarter = N_REP // 4
    shuffled = jax.random.permutation(jax.random.fold_in(key, 19), N_REP).astype(jnp.int32)
    last_pair = quarter * ROWS // 2 - 1
    wanted = quarter + last_pair % quarter
    current = jnp.argsort(shuffled)[N_REP - 1]
    order = shuffled.at[current].set(shuffled[wanted]).at[wanted].set(N_REP - 1)
    ranks = jnp.argsort(order)
    replica = jnp.arange(N_REP * ROWS, dtype=jnp.int32) // ROWS
    inner = jnp.arange(N_REP * ROWS, dtype=jnp.int32) % ROWS
    position = ranks[replica]
    moved = position < quarter
    serial = position * ROWS + inner
    pair = serial // 2
    target = order[quarter + pair % quarter]
    moved_slot = target * SLOTS + ROWS + 2 * (pair // quarter) + serial % 2
    kept_slot = replica * SLOTS + inner
    return jnp.where(moved, moved_slot, kept_slot).astype(jnp.int32)


def draw_queries(key, part):
    base = jax.random.normal(jax.random.fold_in(key, 29), (N_REP * ROWS, 2, HEADS, HEAD_SIZE), jnp.float32)
    return base.reshape(N_REP * ROWS, 2, HEADS * HEAD_SIZE).astype(jnp.bfloat16)


def level_of(stream_key, extent, pieces, least, largest):
    gain, own = 1.0, jax.random.fold_in(stream_key, 6)
    for dim, parts in pieces:
        steps = jnp.exp(jax.random.uniform(jax.random.fold_in(own, dim), (parts,), jnp.float32, least / len(pieces), largest / len(pieces)))
        gain = gain * jnp.repeat(steps, extent[dim] // parts).reshape([-1 if axis == dim else 1 for axis in range(len(extent))])
    return gain


def length_profile(number_of, total, bound, skew):
    loads = [(1 << 20) // math.isqrt(rank ** skew) + 1 for rank in range(2, number_of + 1)]
    rest, holding = total - bound - (number_of - 1), [1] * (number_of - 1)
    while rest > 0:
        candidates = [i for i in range(number_of - 1) if holding[i] < bound]
        pool, budget = sum([loads[i] for i in candidates]), rest
        for i in candidates:
            more = min(bound - holding[i], max(1, budget * loads[i] // pool), rest)
            holding[i] = holding[i] + more
            rest = rest - more
    return np.array([bound] + holding)


def uneven_parts(stream_key, number_of, total, bound, skew):
    if number_of == 2:
        one = jax.random.randint(stream_key, (), max(1, total - bound), min(bound, total - 1) + 1)
        return jnp.stack([one, total - one])
    sizes = jnp.asarray(length_profile(number_of, total, bound, skew), jnp.int32)
    twos = (number_of - 1) // 2
    donor, taker = sizes[1:1 + 2 * twos:2], sizes[2:2 + 2 * twos:2]
    room = jnp.minimum(donor - 1, bound - taker)
    moved = jax.random.randint(jax.random.fold_in(stream_key, 1), (twos,), 0, 1 << 20) % (room + 1)
    sizes = sizes.at[1:1 + 2 * twos:2].set(donor - moved).at[2:2 + 2 * twos:2].set(taker + moved)
    return sizes[jax.random.permutation(jax.random.fold_in(stream_key, 2), number_of)]


def gaussian(own_key, shape, scale, limit, shards=(), kind=jnp.bfloat16):
    drawn = scale * jax.random.normal(own_key, shape, jnp.float32)
    if shards:
        drawn = drawn * level_of(own_key, shape, shards, -0.22, 0.18)
    return jnp.clip(drawn, -limit, limit).astype(kind)


def setup_inputs(seed: int = 0) -> dict:
    arg_keys = jax.random.split(jax.random.key(seed), 14)
    return {
        "hidden": gaussian(arg_keys[0], (N_REP * ROWS, 2, MODEL_WIDTH), 1.0, 6.0, ((0, 32),)),
        "queries": draw_queries(jax.random.fold_in(arg_keys[13], 71), 0),
        "key_weight": gaussian(arg_keys[2], (MODEL_WIDTH, KEY_VALUE_HEADS * HEAD_SIZE), MODEL_WIDTH ** -0.5, 0.0625, ((1, 8),)),
        "value_weight": gaussian(arg_keys[3], (MODEL_WIDTH, KEY_VALUE_HEADS * HEAD_SIZE), MODEL_WIDTH ** -0.5, 0.0625, ((1, 8),)),
        "adapter_down_weight": gaussian(arg_keys[4], (ADAPTER_TOTAL, MODEL_WIDTH, ADAPTER_RANK), MODEL_WIDTH ** -0.5, 0.0625, ((0, 32), (1, 8))),
        "adapter_up_weight": gaussian(arg_keys[5], (ADAPTER_TOTAL, ADAPTER_RANK, KEY_VALUE_HEADS * HEAD_SIZE), ADAPTER_RANK ** -0.5, 0.75, ((0, 32), (2, 8))),
        "row_adapter_index": draw_row_adapter_index(jax.random.fold_in(arg_keys[13], 71), 0),
        "adapter_home_slot": draw_adapter_home_slot(jax.random.fold_in(arg_keys[13], 71), 0),
        "row_page_table": draw_row_page_table(jax.random.fold_in(arg_keys[13], 71), 0),
        "lengths": jax.vmap(lambda own: uneven_parts(own, ROWS, 5 * ROWS * MAXLEN // 8, MAXLEN, 1))(jax.random.split(arg_keys[9], N_REP)).reshape((N_REP, ROWS)).astype(jnp.int32),
        "row_serving_slot": draw_row_serving_slot(jax.random.fold_in(arg_keys[13], 71), 0),
        "paged_key_cache": draw_paged_key_cache(jax.random.fold_in(arg_keys[13], 71), 0),
        "paged_value_cache": gaussian(arg_keys[12], (N_REP * POOL, PAGE, KEY_VALUE_HEADS * HEAD_SIZE), 1.0, 6.0, ((0, 32), (2, 8))),
    }


rope_base = 1000000.0
adapter_scale = 0.5


def rotate(keys, positions, width):
    half = width // 2
    freqs = rope_base ** (-2.0 * jnp.arange(half, dtype=jnp.float32) / width)
    angles = positions[..., None] * freqs
    first = keys[..., :half]
    second = keys[..., half:]
    cosine = jnp.cos(angles)
    sine = jnp.sin(angles)
    return jnp.concatenate([first * cosine - second * sine, second * cosine + first * sine], axis=-1)


def reference(hidden, queries, key_weight, value_weight, adapter_down_weight, adapter_up_weight, row_adapter_index, adapter_home_slot, row_page_table, lengths, row_serving_slot, paged_key_cache, paged_value_cache):
    row_total_count = N_REP * ROWS
    group = HEADS // KEY_VALUE_HEADS
    cached_len = lengths.reshape(-1)
    flat = hidden.reshape(row_total_count * 2, MODEL_WIDTH)
    new_keys = jnp.dot(flat, key_weight, preferred_element_type=jnp.float32).reshape(row_total_count, 2, KEY_VALUE_HEADS, HEAD_SIZE)
    positions = (cached_len[:, None] + jnp.arange(2, dtype=jnp.int32)[None, :]).astype(jnp.float32)
    new_keys = rotate(new_keys, positions[:, :, None], HEAD_SIZE).astype(jnp.bfloat16)
    plain_values = jnp.dot(flat, value_weight, preferred_element_type=jnp.float32).reshape(row_total_count, 2, KEY_VALUE_HEADS * HEAD_SIZE)
    home_slot = adapter_home_slot[row_adapter_index]

    def adapter_value_term(item):
        incoming_rows, serving_slot = item
        reduced_input = jnp.dot(incoming_rows, adapter_down_weight[serving_slot], preferred_element_type=jnp.float32).astype(jnp.bfloat16)
        return jnp.dot(reduced_input, adapter_up_weight[serving_slot], preferred_element_type=jnp.float32)

    adapter_correction_terms = lax.map(adapter_value_term, (hidden, home_slot))
    fresh_values = (plain_values + adapter_scale * adapter_correction_terms).astype(jnp.bfloat16).reshape(row_total_count, 2, KEY_VALUE_HEADS, HEAD_SIZE)
    replica = jnp.arange(row_total_count, dtype=jnp.int32) // ROWS
    pages = (replica[:, None] * POOL + row_page_table).astype(jnp.int32)
    causal = jnp.arange(2)[None, :] <= jnp.arange(2)[:, None]

    def attend(item):
        query_row, keys_new, values_new, page_row, cached = item
        keys_old = paged_key_cache[page_row].astype(jnp.float32).reshape(MAXLEN, KEY_VALUE_HEADS, HEAD_SIZE)
        values_old = paged_value_cache[page_row].astype(jnp.float32).reshape(MAXLEN, KEY_VALUE_HEADS, HEAD_SIZE)
        query_heads = query_row.astype(jnp.float32).reshape(2, KEY_VALUE_HEADS, group, HEAD_SIZE)
        scale = HEAD_SIZE ** -0.5
        old_scores = jnp.einsum("tkgd,jkd->tkgj", query_heads, keys_old) * scale
        seen = jnp.arange(MAXLEN) < cached
        old_scores = jnp.where(seen[None, None, None, :], old_scores, -jnp.inf)
        new_scores = jnp.einsum("tkgd,skd->tkgs", query_heads, keys_new.astype(jnp.float32)) * scale
        new_scores = jnp.where(causal[:, None, None, :], new_scores, -jnp.inf)
        peak = jnp.maximum(old_scores.max(-1), new_scores.max(-1))[..., None]
        old_exp = jnp.exp(old_scores - peak)
        new_exp = jnp.exp(new_scores - peak)
        total = (old_exp.sum(-1) + new_exp.sum(-1))[..., None]
        old_weights = (old_exp / total).astype(jnp.bfloat16).astype(jnp.float32)
        new_weights = (new_exp / total).astype(jnp.bfloat16).astype(jnp.float32)
        mixed = jnp.einsum("tkgj,jkd->tkgd", old_weights, values_old)
        mixed = mixed + jnp.einsum("tkgs,skd->tkgd", new_weights, values_new.astype(jnp.float32))
        return mixed.astype(jnp.bfloat16).reshape(2, HEADS * HEAD_SIZE)

    served = lax.map(attend, (queries, new_keys, fresh_values, pages, cached_len))
    result = jnp.zeros((N_REP * SLOTS, 2, HEADS * HEAD_SIZE), jnp.bfloat16).at[row_serving_slot].set(served)
    return result
```

```python
import functools
import math

import jax
import jax.numpy as jnp
from jax import lax
from jax.experimental import pallas as pl
from jax.experimental.pallas import tpu as pltpu
from jax.sharding import PartitionSpec as P

MESH = pl.DeviceIdType.MESH
F32, BF16, I32 = jnp.float32, jnp.bfloat16, jnp.int32

NX, NZ, TP = 4, 8, 8
NREP = NX * NZ
ROWS, SLOTS, ADP, RANK = 8, 16, 16, 64
LANES = 128
CHUNKS = 64
NT = (((1,), (1,)), ((), ()))
LOG_BASE = math.log(1000000.0)


def kernel(
    hid, qin, wk, wv, dn, up, ridx, home, table, length, serve, kc, vc,
    out,
    hidv, qv, wkv, wvv, dnv, upv, kv, vv, ridx_s, home_s, table_s, length_s, serve_s,
    hf, xl, sb, arr, af, xs, mb, mrec, tb, trec, cs, crec, mixed, wn0s, wn1s, nkf, pvs, served, sb4, grec,
    idx_s, code_s, in_sem, send_sem, recv_sem,
):
    me = lax.axis_index("rep")
    tp = lax.axis_index("tp")
    mx, mz = me // NZ, me % NZ

    def far(a):
        return ((mx + 2 + a % NX) % NX) * NZ + (mz + 4 + a // NX) % NZ

    def peers(do):
        def step(a, carry):
            do(far(a))
            return carry

        lax.fori_loop(0, 18, step, 0)
        lax.fori_loop(19, 32, step, 0)

    def tp_peers(do):
        def step(a, carry):
            do((tp + a) % TP)
            return carry

        lax.fori_loop(1, TP, step, 0)

    bar = pltpu.get_barrier_semaphore()
    peers(lambda d: pl.semaphore_signal(bar, inc=1, device_id=(d, tp), device_id_type=MESH))
    tp_peers(lambda d: pl.semaphore_signal(bar, inc=1, device_id=(me, d), device_id_type=MESH))

    pairs = [
        (ridx, ridx_s), (home, home_s), (serve, serve_s), (hid, hidv), (length, length_s), (table, table_s),
        (wk, wkv), (qin, qv), (kc, kv), (vc, vv), (wv, wvv), (dn, dnv), (up, upv),
    ]
    loads = [pltpu.make_async_copy(s, d, in_sem.at[n]) for n, (s, d) in enumerate(pairs)]
    for c in loads:
        c.start()
    (l_ridx, l_home, l_serve, l_hid, l_len, l_tab, l_wk, l_q, l_k, l_v, l_wv, l_dn, l_up) = loads

    l_ridx.wait()
    l_home.wait()
    l_serve.wait()
    homes = [home_s[ridx_s[i]] for i in range(ROWS)]
    owners = [h // ADP for h in homes]
    slots = [serve_s[i] for i in range(ROWS)]
    lane1 = lax.broadcasted_iota(I32, (1, LANES), 1)
    meta = jnp.zeros((1, LANES), I32)
    for i in range(ROWS):
        meta = jnp.where(lane1 == i, homes[i], meta)
        meta = jnp.where(lane1 == ROWS + i, slots[i], meta)
    mb[...] = meta
    l_hid.wait()
    mine = pl.multiple_of(tp * 16, 16)

    def fill(d, carry):
        row = jnp.int32(0)
        for i in range(1, ROWS):
            row = jnp.where(owners[i] == d, i, row)
        sb[d] = hidv[row, pl.ds(mine, 16), :]
        return carry

    lax.fori_loop(0, NREP, fill, 0)

    pl.semaphore_wait(bar, NREP - 1 + TP - 1)

    def exchange(src, dst, n):
        def one(d):
            pltpu.make_async_remote_copy(
                src(d), dst.at[me], send_sem.at[n], recv_sem.at[n], device_id=(d, tp), device_id_type=MESH
            ).start()

        peers(one)
        pltpu.make_async_copy(src(me), dst.at[me], recv_sem.at[n]).start()

    def received(dst, n):
        pltpu.make_async_copy(dst, dst, recv_sem.at[n]).wait()

    exchange(lambda d: sb.at[d], arr, 0)
    exchange(lambda d: mb, mrec, 1)

    hf[...] = hidv[...].reshape(ROWS * LANES, LANES).astype(F32)
    for c in range(CHUNKS):
        both = [hf[pl.ds(2 * c + t, ROWS, stride=LANES), :] for t in range(2)]
        xl[:, c * LANES : (c + 1) * LANES] = jnp.concatenate(both, axis=0).astype(BF16)
    l_wk.wait()
    new_keys = jnp.dot(xl[...], wkv[...], preferred_element_type=F32)
    l_len.wait()
    row16 = lax.broadcasted_iota(I32, (2 * ROWS, LANES), 0)
    lane16 = lax.broadcasted_iota(I32, (2 * ROWS, LANES), 1)
    position = jnp.zeros((2 * ROWS, LANES), I32)
    for i in range(ROWS):
        for t in range(2):
            position = jnp.where(row16 == t * ROWS + i, length_s[0, i] + t, position)
    half = (lane16 % (LANES // 2)).astype(F32)
    angle = position.astype(F32) * jnp.exp(half * (-2.0 * LOG_BASE / LANES))
    turned = pltpu.roll(new_keys, LANES // 2, 1)
    sine = jnp.where(lane16 < LANES // 2, -jnp.sin(angle), jnp.sin(angle))
    nkf[...] = (new_keys * jnp.cos(angle) + turned * sine).astype(BF16).astype(F32)
    l_wv.wait()
    pvs[...] = jnp.dot(xl[...], wvv[...], preferred_element_type=F32)

    l_tab.wait()
    l_q.wait()
    l_k.wait()
    l_v.wait()
    scale = LANES ** (-0.5)
    span = ROWS * LANES
    token = lax.broadcasted_iota(I32, (16, 1), 0) % 2
    place = lax.broadcasted_iota(I32, (16, span), 1)

    def attend(r, carry):
        q = qv[r]
        pages = [table_s[r, n] for n in range(8)]
        keys = jnp.concatenate([kv[p] for p in pages], axis=0)
        old = lax.dot_general(q, keys, NT, preferred_element_type=F32) * scale
        old = jnp.where(place < length_s[0, r], old, -jnp.inf)
        qf = q.astype(F32)
        new0 = jnp.sum(qf * nkf[pl.ds(r, 1), :], axis=-1, keepdims=True) * scale
        new1 = jnp.sum(qf * nkf[pl.ds(ROWS + r, 1), :], axis=-1, keepdims=True) * scale
        new1 = jnp.where(token == 1, new1, -jnp.inf)
        peak = jnp.maximum(jnp.max(old, axis=-1, keepdims=True), jnp.maximum(new0, new1))
        eo, e0, e1 = jnp.exp(old - peak), jnp.exp(new0 - peak), jnp.exp(new1 - peak)
        total = jnp.sum(eo, axis=-1, keepdims=True) + e0 + e1
        weights = (eo / total).astype(BF16)
        values = jnp.concatenate([vv[p] for p in pages], axis=0)
        mixed[r] = jnp.dot(weights, values, preferred_element_type=F32)
        wn0s[r] = jnp.broadcast_to((e0 / total).astype(BF16).astype(F32), (16, LANES))
        wn1s[r] = jnp.broadcast_to((e1 / total).astype(BF16).astype(F32), (16, LANES))
        return carry

    lax.fori_loop(0, ROWS, attend, 0)

    targets = [s // SLOTS for s in slots]

    def order(d, carry):
        count, first, second = jnp.int32(0), jnp.int32(0), jnp.int32(0)
        for i in range(ROWS):
            here = targets[i] == d
            first = jnp.where(here & (count == 0), i, first)
            second = jnp.where(here & (count == 1), i, second)
            count = count + here.astype(I32)
        idx_s[d, 0] = first
        idx_s[d, 1] = second
        return carry

    lax.fori_loop(0, NREP, order, 0)

    received(mrec, 1)
    known = mrec[:, 0, :]
    lane32 = lax.broadcasted_iota(I32, (NREP, LANES), 1)
    own = ((known // ADP) == me) & (lane32 < ROWS)
    within = jnp.sum(jnp.where(own, (known % ADP).astype(F32), 0.0), axis=-1, keepdims=True).astype(I32)
    pick = jnp.concatenate([within, within], axis=0)
    block = lax.broadcasted_iota(I32, (2 * NREP, ADP * RANK), 1) // RANK
    chosen = block == pick
    received(arr, 0)
    l_dn.wait()
    af[...] = arr[...].reshape(NREP * 16, LANES).astype(F32)
    for c in range(8):
        for t in range(2):
            piece = af[pl.ds(2 * c + t, NREP, stride=16), :]
            xs[t * NREP : (t + 1) * NREP, c * LANES : (c + 1) * LANES] = piece.astype(BF16)
    every = lax.dot_general(xs[...], dnv[...].reshape(ADP * RANK, 8 * LANES), NT, preferred_element_type=F32)
    every = jnp.where(chosen, every, 0.0)
    folded = every[:, :LANES]
    for v in range(1, 8):
        folded = folded + every[:, v * LANES : (v + 1) * LANES]
    folded = folded + pltpu.roll(folded, RANK, 1)
    tb[...] = jnp.where(lane32 < RANK, folded[:NREP], folded[NREP:])

    def to_tp(d):
        pltpu.make_async_remote_copy(
            tb, trec.at[tp], send_sem.at[2], recv_sem.at[2], device_id=(me, d), device_id_type=MESH
        ).start()

    tp_peers(to_tp)
    pltpu.make_async_copy(tb, trec.at[tp], recv_sem.at[2]).start()

    target = known // SLOTS
    rank = jnp.zeros((NREP, LANES), I32)
    for back in range(1, ROWS):
        same = (pltpu.roll(target, back, 1) == target) & (lane32 >= ROWS + back)
        rank = rank + same.astype(I32)
    code = lax.broadcasted_iota(I32, (NREP, LANES), 0) * 2 + rank
    serving = (lane32 >= ROWS) & (lane32 < 2 * ROWS)
    for n in range(ROWS):
        hit = serving & (known == me * SLOTS + ROWS + n)
        code_s[n] = jnp.max(jnp.where(hit, code, -1))

    received(trec, 2)
    l_up.wait()
    low = trec[0]
    for n in range(1, TP):
        low = low + trec[n]
    low = low.astype(BF16).astype(F32)
    other = pltpu.roll(low, RANK, 1)
    spread = jnp.concatenate(
        [jnp.where(lane32 < RANK, low, other), jnp.where(lane32 < RANK, other, low)], axis=0
    )
    wide = jnp.where(chosen, jnp.concatenate([spread] * 8, axis=1), 0.0).astype(BF16)
    term = jnp.dot(wide, upv[...], preferred_element_type=F32)
    cs[:, 0, :] = term[:NREP]
    cs[:, 1, :] = term[NREP:]
    exchange(lambda d: cs.at[d], crec, 3)
    received(crec, 3)

    for r in range(ROWS):
        back = crec[owners[r]]
        value0 = (pvs[r : r + 1, :] + 0.5 * back[0:1]).astype(BF16).astype(F32)
        value1 = (pvs[ROWS + r : ROWS + r + 1, :] + 0.5 * back[1:2]).astype(BF16).astype(F32)
        served[r] = (mixed[r] + wn0s[r] * value0 + wn1s[r] * value1).astype(BF16)

    def moved(d, carry):
        sb4[d, 0] = served[idx_s[d, 0]]
        sb4[d, 1] = served[idx_s[d, 1]]
        return carry

    lax.fori_loop(0, NREP, moved, 0)
    exchange(lambda d: sb4.at[d], grec, 4)
    for r in range(ROWS):
        kept = slots[r] == me * SLOTS + r
        out[r] = jnp.where(kept, served[r], jnp.zeros((16, LANES), BF16))
    received(grec, 4)
    for n in range(ROWS):
        at = code_s[n]
        safe = jnp.clip(at, 0, 2 * NREP - 1)
        row = grec[safe // 2, safe % 2]
        out[ROWS + n] = jnp.where(at >= 0, row, jnp.zeros((16, LANES), BF16))

    def sent(ref, n):
        pltpu.make_async_copy(ref, ref, send_sem.at[n]).wait()

    sent(sb.at[pl.ds(0, NREP - 1)], 0)
    sent(mrec.at[pl.ds(0, NREP - 1)], 1)
    sent(trec.at[pl.ds(0, TP - 1)], 2)
    sent(cs.at[pl.ds(0, NREP - 1)], 3)
    sent(sb4.at[pl.ds(0, NREP - 1)], 4)


def shards(hidden, queries, wk, wv, down, up, ridx, home, table, lengths, serve, kc, vc):
    hid = hidden.reshape(ROWS, 2, CHUNKS, LANES).transpose(0, 2, 1, 3).reshape(ROWS, LANES, LANES)
    qin = queries.reshape(ROWS, 2, 8, LANES).transpose(0, 2, 1, 3).reshape(ROWS, 16, LANES)
    dn = jnp.swapaxes(down, 1, 2)
    upr = up.reshape(ADP * RANK, LANES)
    vmem, smem = pltpu.VMEM, pltpu.SMEM
    scratch = [
        vmem((ROWS, LANES, LANES), BF16), vmem((ROWS, 16, LANES), BF16), vmem((8192, LANES), BF16), vmem((8192, LANES), BF16),
        vmem((ADP, RANK, 1024), BF16), vmem((ADP * RANK, LANES), BF16), vmem((64, LANES, LANES), BF16), vmem((64, LANES, LANES), BF16),
        smem((8,), I32), smem((512,), I32), smem((8, 8), I32), smem((1, 8), I32), smem((8,), I32),
        vmem((ROWS * LANES, LANES), F32), vmem((16, 8192), BF16),
        vmem((NREP, 16, LANES), BF16), vmem((NREP, 16, LANES), BF16),
        vmem((NREP * 16, LANES), F32), vmem((2 * NREP, 1024), BF16),
        vmem((1, LANES), I32), vmem((NREP, 1, LANES), I32),
        vmem((NREP, LANES), F32), vmem((TP, NREP, LANES), F32),
        vmem((NREP, 2, LANES), F32), vmem((NREP, 2, LANES), F32),
        vmem((ROWS, 16, LANES), F32), vmem((ROWS, 16, LANES), F32), vmem((ROWS, 16, LANES), F32),
        vmem((16, LANES), F32), vmem((16, LANES), F32), vmem((ROWS, 16, LANES), BF16),
        vmem((NREP, 2, 16, LANES), BF16), vmem((NREP, 2, 16, LANES), BF16),
        smem((NREP, 2), I32), smem((ROWS,), I32),
        pltpu.SemaphoreType.DMA((13,)), pltpu.SemaphoreType.DMA((5,)), pltpu.SemaphoreType.DMA((5,)),
    ]
    result = pl.pallas_call(
        kernel,
        out_shape=jax.ShapeDtypeStruct((SLOTS, 16, LANES), BF16),
        in_specs=[pl.BlockSpec(memory_space=pltpu.HBM)] * 13,
        out_specs=pl.BlockSpec(memory_space=pltpu.VMEM),
        scratch_shapes=scratch,
        compiler_params=pltpu.CompilerParams(
            collective_id=0, has_side_effects=True, vmem_limit_bytes=67043328
        ),
        name="decode",
    )(hid, qin, wk, wv, dn, upr, ridx, home, table, lengths, serve, kc, vc)
    return result.reshape(SLOTS, 8, 2, LANES).transpose(0, 2, 1, 3).reshape(SLOTS, 2, 1024)


def solution(mesh):
    placed = (
        P("rep", None, None),
        P("rep", None, "tp"),
        P(None, "tp"),
        P(None, "tp"),
        P("rep", "tp", None),
        P("rep", None, "tp"),
        P("rep"),
        P(),
        P("rep", None),
        P("rep", None),
        P("rep"),
        P("rep", None, "tp"),
        P("rep", None, "tp"),
    )
    return jax.shard_map(
        shards, mesh=mesh, in_specs=placed, out_specs=P("rep", None, "tp"), check_vma=False
    )
```

```python
import functools
import math

import jax
import jax.numpy as jnp
from jax import lax
from jax.experimental import pallas as pl
from jax.experimental.pallas import tpu as pltpu
from jax.sharding import PartitionSpec as P

MESH = pl.DeviceIdType.MESH
F32, BF16, I32 = jnp.float32, jnp.bfloat16, jnp.int32

NX, NZ, TP = 4, 8, 8
NREP = NX * NZ
ROWS, SLOTS, ADP, RANK = 8, 16, 16, 64
LANES = 128
CHUNKS = 64
NT = (((1,), (1,)), ((), ()))
LOG_BASE = math.log(1000000.0)


def kernel(
    hid, qin, wk, wv, dn, up, ridx, home, table, length, serve, kc, vc,
    out,
    hidv, qv, wkv, wvv, dnv, upv, kv, vv, ridx_s, home_s, table_s, length_s, serve_s,
    hf, xl, sb, arr, af, xs, mb, mrec, tb, trec, cs, crec, mixed, wn0s, wn1s, nkf, pvs, plain, pair_a, pair_b, sb4, grec,
    route, sb3, mvrec, base, gain0, gain1, tab, tab_s, code_s, in_sem, send_sem, recv_sem,
):
    me = lax.axis_index("rep")
    tp = lax.axis_index("tp")
    mx, mz = me // NZ, me % NZ

    def far(a):
        return ((mx + 2 + a % NX) % NX) * NZ + (mz + 4 + a // NX) % NZ

    def peers(do):
        def step(a, carry):
            do(far(a))
            return carry

        lax.fori_loop(0, 18, step, 0)
        lax.fori_loop(19, 32, step, 0)

    def tp_peers(do):
        def step(a, carry):
            do((tp + a) % TP)
            return carry

        lax.fori_loop(1, TP, step, 0)

    bar = pltpu.get_barrier_semaphore()
    peers(lambda d: pl.semaphore_signal(bar, inc=1, device_id=(d, tp), device_id_type=MESH))
    tp_peers(lambda d: pl.semaphore_signal(bar, inc=1, device_id=(me, d), device_id_type=MESH))

    pairs = [
        (ridx, ridx_s), (home, home_s), (serve, serve_s), (hid, hidv), (length, length_s), (table, table_s),
        (wk, wkv), (qin, qv), (kc, kv), (vc, vv), (wv, wvv), (dn, dnv), (up, upv),
    ]
    loads = [pltpu.make_async_copy(s, d, in_sem.at[n]) for n, (s, d) in enumerate(pairs)]
    for c in loads:
        c.start()
    (l_ridx, l_home, l_serve, l_hid, l_len, l_tab, l_wk, l_q, l_k, l_v, l_wv, l_dn, l_up) = loads

    l_ridx.wait()
    l_home.wait()
    l_serve.wait()
    homes = [home_s[ridx_s[i]] for i in range(ROWS)]
    owners = [h // ADP for h in homes]
    slots = [serve_s[i] for i in range(ROWS)]
    lane1 = lax.broadcasted_iota(I32, (1, LANES), 1)
    meta = jnp.zeros((1, LANES), I32)
    for i in range(ROWS):
        meta = jnp.where(lane1 == i, homes[i], meta)
        meta = jnp.where(lane1 == ROWS + i, slots[i], meta)
    mb[...] = meta
    l_hid.wait()
    mine = pl.multiple_of(tp * 16, 16)

    targets = [s // SLOTS for s in slots]
    none = jnp.zeros((1, LANES), I32)
    to_home, first, second, count = none, none, none, none
    for i in range(ROWS):
        to_home = jnp.where(lane1 == owners[i], i, to_home)
        here = lane1 == targets[i]
        first = jnp.where(here & (count == 0), i, first)
        second = jnp.where(here & (count == 1), i, second)
        count = count + here.astype(I32)
    tab[...] = jnp.zeros((8, LANES), I32)
    tab[0:1, :] = to_home
    tab[1:2, :] = first
    tab[2:3, :] = second
    to_smem = pltpu.make_async_copy(tab, tab_s, in_sem.at[13])
    to_smem.start()
    to_smem.wait()

    def fill(d, carry):
        sb[d] = hidv[tab_s[0, d], pl.ds(mine, 16), :]
        return carry

    lax.fori_loop(0, NREP, fill, 0)

    pl.semaphore_wait(bar, NREP - 1 + TP - 1)

    def exchange(src, dst, n):
        def one(d):
            pltpu.make_async_remote_copy(
                src(d), dst.at[me], send_sem.at[n], recv_sem.at[n], device_id=(d, tp), device_id_type=MESH
            ).start()

        peers(one)
        pltpu.make_async_copy(src(me), dst.at[me], recv_sem.at[n]).start()

    def received(dst, n):
        pltpu.make_async_copy(dst, dst, recv_sem.at[n]).wait()

    exchange(lambda d: sb.at[d], arr, 0)
    exchange(lambda d: mb, mrec, 1)

    hf[...] = hidv[...].reshape(ROWS * LANES, LANES).astype(F32)
    for c in range(CHUNKS):
        both = [hf[pl.ds(2 * c + t, ROWS, stride=LANES), :] for t in range(2)]
        xl[:, c * LANES : (c + 1) * LANES] = jnp.concatenate(both, axis=0).astype(BF16)
    l_wk.wait()
    new_keys = jnp.dot(xl[...], wkv[...], preferred_element_type=F32)
    l_len.wait()
    row16 = lax.broadcasted_iota(I32, (2 * ROWS, LANES), 0)
    lane16 = lax.broadcasted_iota(I32, (2 * ROWS, LANES), 1)
    position = jnp.zeros((2 * ROWS, LANES), I32)
    for i in range(ROWS):
        for t in range(2):
            position = jnp.where(row16 == t * ROWS + i, length_s[0, i] + t, position)
    half = (lane16 % (LANES // 2)).astype(F32)
    angle = position.astype(F32) * jnp.exp(half * (-2.0 * LOG_BASE / LANES))
    turned = pltpu.roll(new_keys, LANES // 2, 1)
    sine = jnp.where(lane16 < LANES // 2, -jnp.sin(angle), jnp.sin(angle))
    nkf[...] = (new_keys * jnp.cos(angle) + turned * sine).astype(BF16).astype(F32)
    l_wv.wait()
    pvs[...] = jnp.dot(xl[...], wvv[...], preferred_element_type=F32)

    l_tab.wait()
    l_q.wait()
    l_k.wait()
    l_v.wait()
    scale = LANES ** (-0.5)
    span = ROWS * LANES
    token = lax.broadcasted_iota(I32, (16, 1), 0) % 2
    place = lax.broadcasted_iota(I32, (16, span), 1)

    def attend(r, carry):
        q = qv[r]
        pages = [table_s[r, n] for n in range(8)]
        keys = jnp.concatenate([kv[p] for p in pages], axis=0)
        old = lax.dot_general(q, keys, NT, preferred_element_type=F32) * scale
        old = jnp.where(place < length_s[0, r], old, -jnp.inf)
        qf = q.astype(F32)
        new0 = jnp.sum(qf * nkf[pl.ds(r, 1), :], axis=-1, keepdims=True) * scale
        new1 = jnp.sum(qf * nkf[pl.ds(ROWS + r, 1), :], axis=-1, keepdims=True) * scale
        new1 = jnp.where(token == 1, new1, -jnp.inf)
        peak = jnp.maximum(jnp.max(old, axis=-1, keepdims=True), jnp.maximum(new0, new1))
        eo, e0, e1 = jnp.exp(old - peak), jnp.exp(new0 - peak), jnp.exp(new1 - peak)
        total = jnp.sum(eo, axis=-1, keepdims=True) + e0 + e1
        weights = (eo / total).astype(BF16)
        values = jnp.concatenate([vv[p] for p in pages], axis=0)
        mixed[r] = jnp.dot(weights, values, preferred_element_type=F32)
        w0 = jnp.broadcast_to((e0 / total).astype(BF16).astype(F32), (16, LANES))
        w1 = jnp.broadcast_to((e1 / total).astype(BF16).astype(F32), (16, LANES))
        wn0s[r] = w0
        wn1s[r] = w1
        fresh = w0 * pvs[pl.ds(r, 1), :] + w1 * pvs[pl.ds(ROWS + r, 1), :]
        plain[r] = (mixed[r] + fresh).astype(BF16)
        pair_a[r] = jnp.where(lane16 == 0, w0, jnp.where(lane16 == 1, w1, 0.0)).astype(BF16)
        pair_b[r] = jnp.where(lane16 == 2, w0, jnp.where(lane16 == 3, w1, 0.0)).astype(BF16)
        return carry

    lax.fori_loop(0, ROWS, attend, 0)

    def moved(d, carry):
        one, two = tab_s[1, d], tab_s[2, d]
        sb4[d, 0] = plain[one]
        sb4[d, 1] = plain[two]
        sb4[d, 2] = pair_a[one] + pair_b[two]
        return carry

    lax.fori_loop(0, NREP, moved, 0)
    exchange(lambda d: sb4.at[d], grec, 4)

    received(mrec, 1)
    known = mrec[:, 0, :]
    lane32 = lax.broadcasted_iota(I32, (NREP, LANES), 1)
    own = ((known // ADP) == me) & (lane32 < ROWS)
    within = jnp.sum(jnp.where(own, (known % ADP).astype(F32), 0.0), axis=-1, keepdims=True).astype(I32)
    pick = jnp.concatenate([within, within], axis=0)
    block = lax.broadcasted_iota(I32, (2 * NREP, ADP * RANK), 1) // RANK
    chosen = block == pick
    received(arr, 0)
    l_dn.wait()
    af[...] = arr[...].reshape(NREP * 16, LANES).astype(F32)
    for c in range(8):
        for t in range(2):
            piece = af[pl.ds(2 * c + t, NREP, stride=16), :]
            xs[t * NREP : (t + 1) * NREP, c * LANES : (c + 1) * LANES] = piece.astype(BF16)
    every = lax.dot_general(xs[...], dnv[...].reshape(ADP * RANK, 8 * LANES), NT, preferred_element_type=F32)
    every = jnp.where(chosen, every, 0.0)
    folded = every[:, :LANES]
    for v in range(1, 8):
        folded = folded + every[:, v * LANES : (v + 1) * LANES]
    folded = folded + pltpu.roll(folded, RANK, 1)
    tb[...] = jnp.where(lane32 < RANK, folded[:NREP], folded[NREP:])

    def to_tp(d):
        pltpu.make_async_remote_copy(
            tb, trec.at[tp], send_sem.at[2], recv_sem.at[2], device_id=(me, d), device_id_type=MESH
        ).start()

    tp_peers(to_tp)
    pltpu.make_async_copy(tb, trec.at[tp], recv_sem.at[2]).start()

    target = known // SLOTS
    rank = jnp.zeros((NREP, LANES), I32)
    for back in range(1, ROWS):
        same = (pltpu.roll(target, back, 1) == target) & (lane32 >= ROWS + back)
        rank = rank + same.astype(I32)
    code = lax.broadcasted_iota(I32, (NREP, LANES), 0) * 2 + rank
    serving = (lane32 >= ROWS) & (lane32 < 2 * ROWS)
    for n in range(ROWS):
        hit = serving & (known == me * SLOTS + ROWS + n)
        code_s[n] = jnp.max(jnp.where(hit, code, -1))

    goal = jnp.sum(jnp.where(pltpu.roll(own.astype(I32), ROWS, 1) > 0, known, 0).astype(F32), axis=-1, keepdims=True)
    held = jnp.sum(own.astype(F32), axis=-1, keepdims=True)
    goal = jnp.where(held > 0.0, goal, -1.0)
    goal = jnp.broadcast_to(jnp.concatenate([goal, goal], axis=0), (2 * NREP, LANES)).T[0:1, :]
    line = lax.broadcasted_iota(I32, (NREP * 16, 2 * NREP), 0)
    from_token = lax.broadcasted_iota(I32, (NREP * 16, 2 * NREP), 1) // NREP
    wanted = (line // 16) * SLOTS + ROWS + (line % 16) // 2
    route[...] = jnp.where((goal == wanted.astype(F32)) & (from_token == line % 2), 1.0, 0.0).astype(BF16)

    received(trec, 2)
    l_up.wait()
    low = trec[0]
    for n in range(1, TP):
        low = low + trec[n]
    low = low.astype(BF16).astype(F32)
    other = pltpu.roll(low, RANK, 1)
    spread = jnp.concatenate(
        [jnp.where(lane32 < RANK, low, other), jnp.where(lane32 < RANK, other, low)], axis=0
    )
    wide = jnp.where(chosen, jnp.concatenate([spread] * 8, axis=1), 0.0).astype(BF16)
    term = jnp.dot(wide, upv[...], preferred_element_type=F32)
    cs[:, 0, :] = term[:NREP]
    cs[:, 1, :] = term[NREP:]
    spread_out = jnp.dot(route[...], term.astype(BF16), preferred_element_type=F32)
    sb3[...] = spread_out.astype(BF16).reshape(NREP, 16, LANES)
    exchange(lambda d: sb3.at[d], mvrec, 5)
    exchange(lambda d: cs.at[d], crec, 3)

    received(grec, 4)
    for n in range(ROWS):
        at = code_s[n]
        safe = jnp.clip(at, 0, 2 * NREP - 1)
        pair = grec[safe // 2, 2].astype(F32)
        odd = safe % 2 == 1
        there = at >= 0
        base[n] = jnp.where(there, grec[safe // 2, safe % 2].astype(F32), 0.0)
        gain0[n] = jnp.broadcast_to(jnp.where(odd, pair[:, 2:3], pair[:, 0:1]) * 0.5, (16, LANES))
        gain1[n] = jnp.broadcast_to(jnp.where(odd, pair[:, 3:4], pair[:, 1:2]) * 0.5, (16, LANES))
    received(crec, 3)
    for r in range(ROWS):
        back = crec[owners[r]]
        value0 = (pvs[r : r + 1, :] + 0.5 * back[0:1]).astype(BF16).astype(F32)
        value1 = (pvs[ROWS + r : ROWS + r + 1, :] + 0.5 * back[1:2]).astype(BF16).astype(F32)
        done = (mixed[r] + wn0s[r] * value0 + wn1s[r] * value1).astype(BF16)
        kept = slots[r] == me * SLOTS + r
        out[r] = jnp.where(kept, done, jnp.zeros((16, LANES), BF16))
    received(mvrec, 5)
    extra = mvrec[0].astype(F32)
    for n in range(1, NREP):
        extra = extra + mvrec[n].astype(F32)
    for n in range(ROWS):
        added = gain0[n] * extra[2 * n : 2 * n + 1] + gain1[n] * extra[2 * n + 1 : 2 * n + 2]
        out[ROWS + n] = (base[n] + added).astype(BF16)

    def sent(ref, n):
        pltpu.make_async_copy(ref, ref, send_sem.at[n]).wait()

    sent(sb.at[pl.ds(0, NREP - 1)], 0)
    sent(mrec.at[pl.ds(0, NREP - 1)], 1)
    sent(trec.at[pl.ds(0, TP - 1)], 2)
    sent(cs.at[pl.ds(0, NREP - 1)], 3)
    sent(sb4.at[pl.ds(0, NREP - 1)], 4)
    sent(sb3.at[pl.ds(0, NREP - 1)], 5)


def shards(hidden, queries, wk, wv, down, up, ridx, home, table, lengths, serve, kc, vc):
    hid = hidden.reshape(ROWS, 2, CHUNKS, LANES).transpose(0, 2, 1, 3).reshape(ROWS, LANES, LANES)
    qin = queries.reshape(ROWS, 2, 8, LANES).transpose(0, 2, 1, 3).reshape(ROWS, 16, LANES)
    dn = jnp.swapaxes(down, 1, 2)
    upr = up.reshape(ADP * RANK, LANES)
    vmem, smem = pltpu.VMEM, pltpu.SMEM
    scratch = [
        vmem((ROWS, LANES, LANES), BF16), vmem((ROWS, 16, LANES), BF16), vmem((8192, LANES), BF16), vmem((8192, LANES), BF16),
        vmem((ADP, RANK, 1024), BF16), vmem((ADP * RANK, LANES), BF16), vmem((64, LANES, LANES), BF16), vmem((64, LANES, LANES), BF16),
        smem((8,), I32), smem((512,), I32), smem((8, 8), I32), smem((1, 8), I32), smem((8,), I32),
        vmem((ROWS * LANES, LANES), F32), vmem((16, 8192), BF16),
        vmem((NREP, 16, LANES), BF16), vmem((NREP, 16, LANES), BF16),
        vmem((NREP * 16, LANES), F32), vmem((2 * NREP, 1024), BF16),
        vmem((1, LANES), I32), vmem((NREP, 1, LANES), I32),
        vmem((NREP, LANES), F32), vmem((TP, NREP, LANES), F32),
        vmem((NREP, 2, LANES), F32), vmem((NREP, 2, LANES), F32),
        vmem((ROWS, 16, LANES), F32), vmem((ROWS, 16, LANES), F32), vmem((ROWS, 16, LANES), F32),
        vmem((16, LANES), F32), vmem((16, LANES), F32),
        vmem((ROWS, 16, LANES), BF16), vmem((ROWS, 16, LANES), BF16), vmem((ROWS, 16, LANES), BF16),
        vmem((NREP, 3, 16, LANES), BF16), vmem((NREP, 3, 16, LANES), BF16),
        vmem((NREP * 16, 2 * NREP), BF16), vmem((NREP, 16, LANES), BF16), vmem((NREP, 16, LANES), BF16),
        vmem((ROWS, 16, LANES), F32), vmem((ROWS, 16, LANES), F32), vmem((ROWS, 16, LANES), F32),
        vmem((8, LANES), I32), smem((8, LANES), I32), smem((ROWS,), I32),
        pltpu.SemaphoreType.DMA((14,)), pltpu.SemaphoreType.DMA((6,)), pltpu.SemaphoreType.DMA((6,)),
    ]
    result = pl.pallas_call(
        kernel,
        out_shape=jax.ShapeDtypeStruct((SLOTS, 16, LANES), BF16),
        in_specs=[pl.BlockSpec(memory_space=pltpu.HBM)] * 13,
        out_specs=pl.BlockSpec(memory_space=pltpu.VMEM),
        scratch_shapes=scratch,
        compiler_params=pltpu.CompilerParams(
            collective_id=0, has_side_effects=True, vmem_limit_bytes=67043328
        ),
        name="decode",
    )(hid, qin, wk, wv, dn, upr, ridx, home, table, lengths, serve, kc, vc)
    return result.reshape(SLOTS, 8, 2, LANES).transpose(0, 2, 1, 3).reshape(SLOTS, 2, 1024)


def solution(mesh):
    placed = (
        P("rep", None, None),
        P("rep", None, "tp"),
        P(None, "tp"),
        P(None, "tp"),
        P("rep", "tp", None),
        P("rep", None, "tp"),
        P("rep"),
        P(),
        P("rep", None),
        P("rep", None),
        P("rep"),
        P("rep", None, "tp"),
        P("rep", None, "tp"),
    )
    return jax.shard_map(
        shards, mesh=mesh, in_specs=placed, out_specs=P("rep", None, "tp"), check_vma=False
    )
```

```python
import functools
import math

import jax
import jax.numpy as jnp
from jax import lax
from jax.experimental import pallas as pl
from jax.experimental.pallas import tpu as pltpu
from jax.sharding import PartitionSpec as P

MESH = pl.DeviceIdType.MESH
F32, BF16, I32 = jnp.float32, jnp.bfloat16, jnp.int32

NX, NZ, TP = 4, 8, 8
NREP = NX * NZ
ROWS, SLOTS, ADP, RANK = 8, 16, 16, 64
LANES = 128
CHUNKS = 64
NT = (((1,), (1,)), ((), ()))
LOG_BASE = math.log(1000000.0)
FAR_FIRST = sorted(
    [(x, z) for x in range(NX) for z in range(NZ) if x or z],
    key=lambda o: -(min(o[0], NX - o[0]) + min(o[1], NZ - o[1])),
)


def kernel(
    hid, qin, wk, wv, dn, up, ridx, home, table, length, serve, kc, vc,
    out,
    hidv, qv, wkv, wvv, dnv, upv, kv, vv, ridx_s, home_s, table_s, length_s, serve_s,
    hf, xl, sb, arr, af, xs, mb, mrec, tb, trec, cs, crec, mixed, wn0s, wn1s, nkf, pvs, plain, gains, wb, wrec, sb4, grec,
    route, sb3, mvrec, base, gain0, gain1, tab, tab_s, code_s, line_s, wq, in_sem, send_sem, recv_sem,
):
    me = lax.axis_index("rep")
    tp = lax.axis_index("tp")
    mx, mz = me // NZ, me % NZ

    to_x = [((mx + n) % NX) * NZ for n in range(NX)]
    to_z = [(mz + n) % NZ for n in range(NZ)]

    def peers(do):
        for dx, dz in FAR_FIRST:
            do(to_x[dx] + to_z[dz])

    def tp_peers(do):
        for a in (4, 5, 3, 2, 6, 1, 7):
            do((tp + a) % TP)

    bar = pltpu.get_barrier_semaphore()
    peers(lambda d: pl.semaphore_signal(bar, inc=1, device_id=(d, tp), device_id_type=MESH))
    tp_peers(lambda d: pl.semaphore_signal(bar, inc=1, device_id=(me, d), device_id_type=MESH))

    pairs = [
        (ridx, ridx_s), (home, home_s), (serve, serve_s), (hid, hidv), (length, length_s), (table, table_s),
        (wk, wkv), (wv, wvv), (qin, qv), (kc, kv), (vc, vv), (dn, dnv), (up, upv),
    ]
    loads = [pltpu.make_async_copy(s, d, in_sem.at[n]) for n, (s, d) in enumerate(pairs)]
    for c in loads:
        c.start()
    (l_ridx, l_home, l_serve, l_hid, l_len, l_tab, l_wk, l_wv, l_q, l_k, l_v, l_dn, l_up) = loads

    l_hid.wait()
    hf[...] = hidv[...].reshape(ROWS * LANES, LANES).astype(F32)
    for c in range(CHUNKS):
        both = [hf[pl.ds(2 * c + t, ROWS, stride=LANES), :] for t in range(2)]
        xl[:, c * LANES : (c + 1) * LANES] = jnp.concatenate(both, axis=0).astype(BF16)
    l_ridx.wait()
    l_home.wait()
    l_serve.wait()
    homes = [home_s[ridx_s[i]] for i in range(ROWS)]
    owners = [h // ADP for h in homes]
    slots = [serve_s[i] for i in range(ROWS)]
    lane1 = lax.broadcasted_iota(I32, (1, LANES), 1)
    meta = jnp.zeros((1, LANES), I32)
    for i in range(ROWS):
        meta = jnp.where(lane1 == i, homes[i], meta)
        meta = jnp.where(lane1 == ROWS + i, slots[i], meta)
    mb[...] = meta
    mine = pl.multiple_of(tp * 16, 16)

    targets = [s // SLOTS for s in slots]
    none = jnp.zeros((1, LANES), I32)
    to_home, first, second, count = none, none, none, none
    for i in range(ROWS):
        to_home = jnp.where(lane1 == owners[i], i, to_home)
        here = lane1 == targets[i]
        first = jnp.where(here & (count == 0), i, first)
        second = jnp.where(here & (count == 1), i, second)
        count = count + here.astype(I32)
    tab[...] = jnp.zeros((8, LANES), I32)
    tab[0:1, :] = to_home
    tab[1:2, :] = first
    tab[2:3, :] = second
    to_smem = pltpu.make_async_copy(tab, tab_s, in_sem.at[13])
    to_smem.start()
    l_wk.wait()
    new_keys = jnp.dot(xl[...], wkv[...], preferred_element_type=F32)
    l_len.wait()
    row16 = lax.broadcasted_iota(I32, (2 * ROWS, LANES), 0)
    lane16 = lax.broadcasted_iota(I32, (2 * ROWS, LANES), 1)
    position = jnp.zeros((2 * ROWS, LANES), I32)
    for i in range(ROWS):
        for t in range(2):
            position = jnp.where(row16 == t * ROWS + i, length_s[0, i] + t, position)
    half = (lane16 % (LANES // 2)).astype(F32)
    angle = position.astype(F32) * jnp.exp(half * (-2.0 * LOG_BASE / LANES))
    turned = pltpu.roll(new_keys, LANES // 2, 1)
    sine = jnp.where(lane16 < LANES // 2, -jnp.sin(angle), jnp.sin(angle))
    nkf[...] = (new_keys * jnp.cos(angle) + turned * sine).astype(BF16).astype(F32)
    l_wv.wait()
    pvs[...] = jnp.dot(xl[...], wvv[...], preferred_element_type=F32)

    to_smem.wait()

    def fill(d, carry):
        sb[d] = hidv[tab_s[0, d], pl.ds(mine, 16), :]
        return carry

    lax.fori_loop(0, NREP, fill, 0)

    pl.semaphore_wait(bar, NREP - 1 + TP - 1)

    def exchange(*moves):
        def one(d):
            for src, dst, n in moves:
                pltpu.make_async_remote_copy(
                    src(d), dst.at[me], send_sem.at[n], recv_sem.at[n], device_id=(d, tp), device_id_type=MESH
                ).start()

        peers(one)
        for src, dst, n in moves:
            pltpu.make_async_copy(src(me), dst.at[me], recv_sem.at[n]).start()

    def received(dst, n):
        pltpu.make_async_copy(dst, dst, recv_sem.at[n]).wait()

    exchange((lambda d: sb.at[d], arr, 0), (lambda d: mb, mrec, 1))

    l_tab.wait()
    l_q.wait()
    l_k.wait()
    l_v.wait()
    scale = LANES ** (-0.5)
    span = ROWS * LANES
    token = lax.broadcasted_iota(I32, (16, 1), 0) % 2
    place = lax.broadcasted_iota(I32, (16, span), 1)

    def attend(r, carry):
        q = qv[r]
        pages = [table_s[r, n] for n in range(8)]
        keys = jnp.concatenate([kv[p] for p in pages], axis=0)
        old = lax.dot_general(q, keys, NT, preferred_element_type=F32) * scale
        old = jnp.where(place < length_s[0, r], old, -jnp.inf)
        qf = q.astype(F32)
        new0 = jnp.sum(qf * nkf[pl.ds(r, 1), :], axis=-1, keepdims=True) * scale
        new1 = jnp.sum(qf * nkf[pl.ds(ROWS + r, 1), :], axis=-1, keepdims=True) * scale
        new1 = jnp.where(token == 1, new1, -jnp.inf)
        peak = jnp.maximum(jnp.max(old, axis=-1, keepdims=True), jnp.maximum(new0, new1))
        eo, e0, e1 = jnp.exp(old - peak), jnp.exp(new0 - peak), jnp.exp(new1 - peak)
        total = jnp.sum(eo, axis=-1, keepdims=True) + e0 + e1
        weights = (eo / total).astype(BF16)
        values = jnp.concatenate([vv[p] for p in pages], axis=0)
        mixed[r] = jnp.dot(weights, values, preferred_element_type=F32)
        w0 = jnp.broadcast_to((e0 / total).astype(BF16).astype(F32), (16, LANES))
        w1 = jnp.broadcast_to((e1 / total).astype(BF16).astype(F32), (16, LANES))
        wn0s[r] = w0
        wn1s[r] = w1
        fresh = w0 * pvs[pl.ds(r, 1), :] + w1 * pvs[pl.ds(ROWS + r, 1), :]
        plain[r] = (mixed[r] + fresh).astype(BF16)
        gains[r] = jnp.where(lane16 == 0, w0, w1)
        return carry

    def several(n, carry):
        for u in range(4):
            attend(n * 4 + u, carry)
        return carry

    lax.fori_loop(0, ROWS // 4, several, 0)

    def moved(d, carry):
        one, two = tab_s[1, d], tab_s[2, d]
        sb4[d, 0] = plain[one]
        sb4[d, 1] = plain[two]
        return carry

    wb[...] = gains[...].reshape(ROWS * 16, LANES).T[0:2, :]
    lax.fori_loop(0, NREP, moved, 0)
    exchange((lambda d: sb4.at[d], grec, 4), (lambda d: wb, wrec, 2))

    received(mrec, 1)
    known = mrec[:, 0, :]
    lane32 = lax.broadcasted_iota(I32, (NREP, LANES), 1)
    own = ((known // ADP) == me) & (lane32 < ROWS)
    within = jnp.sum(jnp.where(own, (known % ADP).astype(F32), 0.0), axis=-1, keepdims=True).astype(I32)
    pick = jnp.concatenate([within, within], axis=0)
    block = lax.broadcasted_iota(I32, (2 * NREP, ADP * RANK), 1) // RANK
    chosen = block == pick
    received(arr, 0)
    l_dn.wait()
    af[...] = arr[...].reshape(NREP * 16, LANES).astype(F32)
    for c in range(8):
        for t in range(2):
            piece = af[pl.ds(2 * c + t, NREP, stride=16), :]
            xs[t * NREP : (t + 1) * NREP, c * LANES : (c + 1) * LANES] = piece.astype(BF16)
    every = lax.dot_general(xs[...], dnv[...].reshape(ADP * RANK, 8 * LANES), NT, preferred_element_type=F32)
    every = jnp.where(chosen, every, 0.0)
    folded = every[:, :LANES]
    for v in range(1, 8):
        folded = folded + every[:, v * LANES : (v + 1) * LANES]
    folded = folded + pltpu.roll(folded, RANK, 1)
    tb[...] = jnp.where(lane32 < RANK, folded[:NREP], folded[NREP:])

    def to_tp(d):
        pltpu.make_async_remote_copy(
            tb, trec.at[tp], send_sem.at[6], recv_sem.at[6], device_id=(me, d), device_id_type=MESH
        ).start()

    tp_peers(to_tp)
    pltpu.make_async_copy(tb, trec.at[tp], recv_sem.at[6]).start()

    target = known // SLOTS
    rank = jnp.zeros((NREP, LANES), I32)
    for back in range(1, ROWS):
        same = (pltpu.roll(target, back, 1) == target) & (lane32 >= ROWS + back)
        rank = rank + same.astype(I32)
    code = lax.broadcasted_iota(I32, (NREP, LANES), 0) * 2 + rank
    serving = (lane32 >= ROWS) & (lane32 < 2 * ROWS)
    for n in range(ROWS):
        hit = serving & (known == me * SLOTS + ROWS + n)
        code_s[n] = jnp.max(jnp.where(hit, code, -1))
        line_s[n] = jnp.max(jnp.where(hit, lane32 - ROWS, 0))

    goal = jnp.sum(jnp.where(pltpu.roll(own.astype(I32), ROWS, 1) > 0, known, 0).astype(F32), axis=-1, keepdims=True)
    held = jnp.sum(own.astype(F32), axis=-1, keepdims=True)
    goal = jnp.where(held > 0.0, goal, -1.0)
    goal = jnp.broadcast_to(jnp.concatenate([goal, goal], axis=0), (2 * NREP, LANES)).T[0:1, :]
    line = lax.broadcasted_iota(I32, (NREP * 16, 2 * NREP), 0)
    from_token = lax.broadcasted_iota(I32, (NREP * 16, 2 * NREP), 1) // NREP
    wanted = (line // 16) * SLOTS + ROWS + (line % 16) // 2
    route[...] = jnp.where((goal == wanted.astype(F32)) & (from_token == line % 2), 1.0, 0.0).astype(BF16)

    received(trec, 6)
    l_up.wait()
    low = trec[0]
    for n in range(1, TP):
        low = low + trec[n]
    low = low.astype(BF16).astype(F32)
    other = pltpu.roll(low, RANK, 1)
    spread = jnp.concatenate(
        [jnp.where(lane32 < RANK, low, other), jnp.where(lane32 < RANK, other, low)], axis=0
    )
    wide = jnp.where(chosen, jnp.concatenate([spread] * 8, axis=1), 0.0).astype(BF16)
    term = jnp.dot(wide, upv[...], preferred_element_type=F32)
    cs[:, 0, :] = term[:NREP]
    cs[:, 1, :] = term[NREP:]
    spread_out = jnp.dot(route[...], term.astype(BF16), preferred_element_type=F32)
    sb3[...] = spread_out.astype(BF16).reshape(NREP, 16, LANES)
    exchange((lambda d: sb3.at[d], mvrec, 5), (lambda d: cs.at[d], crec, 3))

    received(grec, 4)
    received(wrec, 2)
    for n in range(ROWS):
        safe = jnp.clip(code_s[n], 0, 2 * NREP - 1)
        shift = (LANES - jnp.clip(line_s[n], 0, ROWS - 1) * 16) % LANES
        wq[2 * n : 2 * n + 2, :] = pltpu.roll(wrec[safe // 2], shift, 1)
    column = wq[...].T[0:16, :] * 0.5
    for n in range(ROWS):
        safe = jnp.clip(code_s[n], 0, 2 * NREP - 1)
        base[n] = jnp.where(code_s[n] >= 0, grec[safe // 2, safe % 2].astype(F32), 0.0)
        gain0[n] = jnp.broadcast_to(column[:, 2 * n : 2 * n + 1], (16, LANES))
        gain1[n] = jnp.broadcast_to(column[:, 2 * n + 1 : 2 * n + 2], (16, LANES))
    received(crec, 3)
    for r in range(ROWS):
        back = crec[owners[r]]
        value0 = (pvs[r : r + 1, :] + 0.5 * back[0:1]).astype(BF16).astype(F32)
        value1 = (pvs[ROWS + r : ROWS + r + 1, :] + 0.5 * back[1:2]).astype(BF16).astype(F32)
        done = (mixed[r] + wn0s[r] * value0 + wn1s[r] * value1).astype(BF16)
        kept = slots[r] == me * SLOTS + r
        out[r] = jnp.where(kept, done, jnp.zeros((16, LANES), BF16))
    received(mvrec, 5)
    extra = mvrec[0].astype(F32)
    for n in range(1, NREP):
        extra = extra + mvrec[n].astype(F32)
    for n in range(ROWS):
        added = gain0[n] * extra[2 * n : 2 * n + 1] + gain1[n] * extra[2 * n + 1 : 2 * n + 2]
        out[ROWS + n] = (base[n] + added).astype(BF16)

    def sent(ref, n):
        pltpu.make_async_copy(ref, ref, send_sem.at[n]).wait()

    sent(sb.at[pl.ds(0, NREP - 1)], 0)
    sent(mrec.at[pl.ds(0, NREP - 1)], 1)
    sent(trec.at[pl.ds(0, TP - 1)], 6)
    sent(wrec.at[pl.ds(0, NREP - 1)], 2)
    sent(cs.at[pl.ds(0, NREP - 1)], 3)
    sent(sb4.at[pl.ds(0, NREP - 1)], 4)
    sent(sb3.at[pl.ds(0, NREP - 1)], 5)


def shards(hidden, queries, wk, wv, down, up, ridx, home, table, lengths, serve, kc, vc):
    hid = hidden.reshape(ROWS, 2, CHUNKS, LANES).transpose(0, 2, 1, 3).reshape(ROWS, LANES, LANES)
    qin = queries.reshape(ROWS, 2, 8, LANES).transpose(0, 2, 1, 3).reshape(ROWS, 16, LANES)
    dn = jnp.swapaxes(down, 1, 2)
    upr = up.reshape(ADP * RANK, LANES)
    vmem, smem = pltpu.VMEM, pltpu.SMEM
    scratch = [
        vmem((ROWS, LANES, LANES), BF16), vmem((ROWS, 16, LANES), BF16), vmem((8192, LANES), BF16), vmem((8192, LANES), BF16),
        vmem((ADP, RANK, 1024), BF16), vmem((ADP * RANK, LANES), BF16), vmem((64, LANES, LANES), BF16), vmem((64, LANES, LANES), BF16),
        smem((8,), I32), smem((512,), I32), smem((8, 8), I32), smem((1, 8), I32), smem((8,), I32),
        vmem((ROWS * LANES, LANES), F32), vmem((16, 8192), BF16),
        vmem((NREP, 16, LANES), BF16), vmem((NREP, 16, LANES), BF16),
        vmem((NREP * 16, LANES), F32), vmem((2 * NREP, 1024), BF16),
        vmem((1, LANES), I32), vmem((NREP, 1, LANES), I32),
        vmem((NREP, LANES), F32), vmem((TP, NREP, LANES), F32),
        vmem((NREP, 2, LANES), F32), vmem((NREP, 2, LANES), F32),
        vmem((ROWS, 16, LANES), F32), vmem((ROWS, 16, LANES), F32), vmem((ROWS, 16, LANES), F32),
        vmem((16, LANES), F32), vmem((16, LANES), F32),
        vmem((ROWS, 16, LANES), BF16), vmem((ROWS, 16, LANES), F32), vmem((2, LANES), F32), vmem((NREP, 2, LANES), F32),
        vmem((NREP, 2, 16, LANES), BF16), vmem((NREP, 2, 16, LANES), BF16),
        vmem((NREP * 16, 2 * NREP), BF16), vmem((NREP, 16, LANES), BF16), vmem((NREP, 16, LANES), BF16),
        vmem((ROWS, 16, LANES), F32), vmem((ROWS, 16, LANES), F32), vmem((ROWS, 16, LANES), F32),
        vmem((8, LANES), I32), smem((8, LANES), I32), smem((ROWS,), I32), smem((ROWS,), I32), vmem((16, LANES), F32),
        pltpu.SemaphoreType.DMA((14,)), pltpu.SemaphoreType.DMA((7,)), pltpu.SemaphoreType.DMA((7,)),
    ]
    result = pl.pallas_call(
        kernel,
        out_shape=jax.ShapeDtypeStruct((SLOTS, 16, LANES), BF16),
        in_specs=[pl.BlockSpec(memory_space=pltpu.HBM)] * 13,
        out_specs=pl.BlockSpec(memory_space=pltpu.VMEM),
        scratch_shapes=scratch,
        compiler_params=pltpu.CompilerParams(
            collective_id=0, has_side_effects=True, vmem_limit_bytes=67043328
        ),
        name="decode",
    )(hid, qin, wk, wv, dn, upr, ridx, home, table, lengths, serve, kc, vc)
    return result.reshape(SLOTS, 8, 2, LANES).transpose(0, 2, 1, 3).reshape(SLOTS, 2, 1024)


def solution(mesh):
    placed = (
        P("rep", None, None),
        P("rep", None, "tp"),
        P(None, "tp"),
        P(None, "tp"),
        P("rep", "tp", None),
        P("rep", None, "tp"),
        P("rep"),
        P(),
        P("rep", None),
        P("rep", None),
        P("rep"),
        P("rep", None, "tp"),
        P("rep", None, "tp"),
    )
    return jax.shard_map(
        shards, mesh=mesh, in_specs=placed, out_specs=P("rep", None, "tp"), check_vma=False
    )
```

```python
import functools
import math

import jax
import jax.numpy as jnp
from jax import lax
from jax.experimental import pallas as pl
from jax.experimental.pallas import tpu as pltpu
from jax.sharding import PartitionSpec as P

MESH = pl.DeviceIdType.MESH
F32, BF16, I32 = jnp.float32, jnp.bfloat16, jnp.int32

NX, NZ, TP = 4, 8, 8
NREP = NX * NZ
ROWS, SLOTS, ADP, RANK = 8, 16, 16, 64
LANES = 128
CHUNKS = 64
NT = (((1,), (1,)), ((), ()))
LOG_BASE = math.log(1000000.0)
FAR_FIRST = sorted(
    [(x, z) for x in range(NX) for z in range(NZ) if x or z],
    key=lambda o: -(min(o[0], NX - o[0]) + min(o[1], NZ - o[1])),
)


def kernel(
    hid, qin, wk, wv, dn, up, ridx, home, table, length, serve, kc, vc,
    out,
    hidv, qv, wkv, wvv, dnv, upv, kv, vv, ridx_s, home_s, table_s, length_s, serve_s,
    hf, xl, sb, arr, af, xs, mb, mrec, tb, trec, cs, crec, mixed, wn0s, wn1s, nkf, pvs, plain, gains, wb, wrec, sb4, grec,
    route, sb3, mvrec, base, gain0, gain1, tab, tab_s, code_s, line_s, wq, in_sem, send_sem, recv_sem,
):
    me = lax.axis_index("rep")
    tp = lax.axis_index("tp")
    mx, mz = me // NZ, me % NZ

    to_x = [((mx + n) % NX) * NZ for n in range(NX)]
    to_z = [(mz + n) % NZ for n in range(NZ)]

    def peers(do):
        for dx, dz in FAR_FIRST:
            do(to_x[dx] + to_z[dz])

    def tp_peers(do):
        for a in (4, 5, 3, 2, 6, 1, 7):
            do((tp + a) % TP)

    bar = pltpu.get_barrier_semaphore()
    peers(lambda d: pl.semaphore_signal(bar, inc=1, device_id=(d, tp), device_id_type=MESH))
    tp_peers(lambda d: pl.semaphore_signal(bar, inc=1, device_id=(me, d), device_id_type=MESH))

    pairs = [
        (ridx, ridx_s), (home, home_s), (serve, serve_s), (hid, hidv), (length, length_s), (table, table_s),
        (wk, wkv), (wv, wvv), (qin, qv), (kc, kv), (vc, vv), (dn, dnv), (up, upv),
    ]
    loads = [pltpu.make_async_copy(s, d, in_sem.at[n]) for n, (s, d) in enumerate(pairs)]
    for c in loads:
        c.start()
    (l_ridx, l_home, l_serve, l_hid, l_len, l_tab, l_wk, l_wv, l_q, l_k, l_v, l_dn, l_up) = loads

    l_hid.wait()
    hf[...] = hidv[...].reshape(ROWS * LANES, LANES).astype(F32)
    for c in range(CHUNKS):
        both = [hf[pl.ds(2 * c + t, ROWS, stride=LANES), :] for t in range(2)]
        xl[:, c * LANES : (c + 1) * LANES] = jnp.concatenate(both, axis=0).astype(BF16)
    l_ridx.wait()
    l_home.wait()
    l_serve.wait()
    homes = [home_s[ridx_s[i]] for i in range(ROWS)]
    owners = [h // ADP for h in homes]
    slots = [serve_s[i] for i in range(ROWS)]
    lane1 = lax.broadcasted_iota(I32, (1, LANES), 1)
    meta = jnp.zeros((1, LANES), I32)
    for i in range(ROWS):
        meta = jnp.where(lane1 == i, homes[i], meta)
        meta = jnp.where(lane1 == ROWS + i, slots[i], meta)
    mb[...] = meta
    mine = pl.multiple_of(tp * 16, 16)

    targets = [s // SLOTS for s in slots]
    none = jnp.zeros((1, LANES), I32)
    to_home, first, second, count = none, none, none, none
    for i in range(ROWS):
        to_home = jnp.where(lane1 == owners[i], i, to_home)
        here = lane1 == targets[i]
        first = jnp.where(here & (count == 0), i, first)
        second = jnp.where(here & (count == 1), i, second)
        count = count + here.astype(I32)
    tab[...] = jnp.zeros((8, LANES), I32)
    tab[0:1, :] = to_home
    tab[1:2, :] = first
    tab[2:3, :] = second
    to_smem = pltpu.make_async_copy(tab, tab_s, in_sem.at[13])
    to_smem.start()
    l_wk.wait()
    new_keys = jnp.dot(xl[...], wkv[...], preferred_element_type=F32)
    l_len.wait()
    row16 = lax.broadcasted_iota(I32, (2 * ROWS, LANES), 0)
    lane16 = lax.broadcasted_iota(I32, (2 * ROWS, LANES), 1)
    position = jnp.zeros((2 * ROWS, LANES), I32)
    for i in range(ROWS):
        for t in range(2):
            position = jnp.where(row16 == t * ROWS + i, length_s[0, i] + t, position)
    half = (lane16 % (LANES // 2)).astype(F32)
    angle = position.astype(F32) * jnp.exp(half * (-2.0 * LOG_BASE / LANES))
    turned = pltpu.roll(new_keys, LANES // 2, 1)
    sine = jnp.where(lane16 < LANES // 2, -jnp.sin(angle), jnp.sin(angle))
    nkf[...] = (new_keys * jnp.cos(angle) + turned * sine).astype(BF16).astype(F32)
    l_wv.wait()
    pvs[...] = jnp.dot(xl[...], wvv[...], preferred_element_type=F32)

    to_smem.wait()

    def fill(d, carry):
        sb[d] = hidv[tab_s[0, d], pl.ds(mine, 16), :]
        return carry

    lax.fori_loop(0, NREP, fill, 0)

    pl.semaphore_wait(bar, NREP - 1 + TP - 1)

    def exchange(*moves):
        def one(d):
            for src, dst, n in moves:
                pltpu.make_async_remote_copy(
                    src(d), dst.at[me], send_sem.at[n], recv_sem.at[n], device_id=(d, tp), device_id_type=MESH
                ).start()

        peers(one)
        for src, dst, n in moves:
            pltpu.make_async_copy(src(me), dst.at[me], recv_sem.at[n]).start()

    def received(dst, n):
        pltpu.make_async_copy(dst, dst, recv_sem.at[n]).wait()

    exchange((lambda d: sb.at[d], arr, 0), (lambda d: mb, mrec, 1))

    l_tab.wait()
    l_q.wait()
    l_k.wait()
    l_v.wait()
    scale = LANES ** (-0.5)
    span = ROWS * LANES
    token = lax.broadcasted_iota(I32, (16, 1), 0) % 2
    place = lax.broadcasted_iota(I32, (16, span), 1)

    def attend(r, carry):
        q = qv[r]
        pages = [table_s[r, n] for n in range(8)]
        keys = jnp.concatenate([kv[p] for p in pages], axis=0)
        old = lax.dot_general(q, keys, NT, preferred_element_type=F32) * scale
        old = jnp.where(place < length_s[0, r], old, -jnp.inf)
        qf = q.astype(F32)
        new0 = jnp.sum(qf * nkf[pl.ds(r, 1), :], axis=-1, keepdims=True) * scale
        new1 = jnp.sum(qf * nkf[pl.ds(ROWS + r, 1), :], axis=-1, keepdims=True) * scale
        new1 = jnp.where(token == 1, new1, -jnp.inf)
        peak = jnp.maximum(jnp.max(old, axis=-1, keepdims=True), jnp.maximum(new0, new1))
        eo, e0, e1 = jnp.exp(old - peak), jnp.exp(new0 - peak), jnp.exp(new1 - peak)
        total = jnp.sum(eo, axis=-1, keepdims=True) + e0 + e1
        weights = (eo / total).astype(BF16)
        values = jnp.concatenate([vv[p] for p in pages], axis=0)
        mixed[r] = jnp.dot(weights, values, preferred_element_type=F32)
        w0 = jnp.broadcast_to((e0 / total).astype(BF16).astype(F32), (16, LANES))
        w1 = jnp.broadcast_to((e1 / total).astype(BF16).astype(F32), (16, LANES))
        wn0s[r] = w0
        wn1s[r] = w1
        fresh = w0 * pvs[pl.ds(r, 1), :] + w1 * pvs[pl.ds(ROWS + r, 1), :]
        plain[r] = (mixed[r] + fresh).astype(BF16)
        gains[r] = jnp.where(lane16 == 0, w0, w1)
        return carry

    def several(n, carry):
        for u in range(4):
            attend(n * 4 + u, carry)
        return carry

    lax.fori_loop(0, ROWS // 4, several, 0)

    def moved(d, carry):
        one, two = tab_s[1, d], tab_s[2, d]
        sb4[d, 0] = plain[one]
        sb4[d, 1] = plain[two]
        return carry

    wb[...] = gains[...].reshape(ROWS * 16, LANES).T[0:2, :]
    lax.fori_loop(0, NREP, moved, 0)
    exchange((lambda d: sb4.at[d], grec, 4), (lambda d: wb, wrec, 2))

    received(mrec, 1)
    known = mrec[:, 0, :]
    lane32 = lax.broadcasted_iota(I32, (NREP, LANES), 1)
    own = ((known // ADP) == me) & (lane32 < ROWS)
    within = jnp.sum(jnp.where(own, (known % ADP).astype(F32), 0.0), axis=-1, keepdims=True).astype(I32)
    pick = jnp.concatenate([within, within], axis=0)
    block = lax.broadcasted_iota(I32, (2 * NREP, ADP * RANK), 1) // RANK
    chosen = block == pick
    received(arr, 0)
    l_dn.wait()
    af[...] = arr[...].reshape(NREP * 16, LANES).astype(F32)
    for c in range(8):
        for t in range(2):
            piece = af[pl.ds(2 * c + t, NREP, stride=16), :]
            xs[t * NREP : (t + 1) * NREP, c * LANES : (c + 1) * LANES] = piece.astype(BF16)
    every = lax.dot_general(xs[...], dnv[...].reshape(ADP * RANK, 8 * LANES), NT, preferred_element_type=F32)
    every = jnp.where(chosen, every, 0.0)
    folded = every[:, :LANES]
    for v in range(1, 8):
        folded = folded + every[:, v * LANES : (v + 1) * LANES]
    folded = folded + pltpu.roll(folded, RANK, 1)
    tb[...] = jnp.where(lane32 < RANK, folded[:NREP], folded[NREP:])

    def to_tp(d):
        pltpu.make_async_remote_copy(
            tb, trec.at[tp], send_sem.at[6], recv_sem.at[6], device_id=(me, d), device_id_type=MESH
        ).start()

    tp_peers(to_tp)
    pltpu.make_async_copy(tb, trec.at[tp], recv_sem.at[6]).start()

    target = known // SLOTS
    rank = jnp.zeros((NREP, LANES), I32)
    for back in range(1, ROWS):
        same = (pltpu.roll(target, back, 1) == target) & (lane32 >= ROWS + back)
        rank = rank + same.astype(I32)
    code = lax.broadcasted_iota(I32, (NREP, LANES), 0) * 2 + rank
    serving = (lane32 >= ROWS) & (lane32 < 2 * ROWS)
    for n in range(ROWS):
        hit = serving & (known == me * SLOTS + ROWS + n)
        code_s[n] = jnp.max(jnp.where(hit, code, -1))
        line_s[n] = jnp.max(jnp.where(hit, lane32 - ROWS, 0))

    goal = jnp.sum(jnp.where(pltpu.roll(own.astype(I32), ROWS, 1) > 0, known, 0).astype(F32), axis=-1, keepdims=True)
    held = jnp.sum(own.astype(F32), axis=-1, keepdims=True)
    goal = jnp.where(held > 0.0, goal, -1.0)
    goal = jnp.broadcast_to(jnp.concatenate([goal, goal], axis=0), (2 * NREP, LANES)).T[0:1, :]
    line = lax.broadcasted_iota(I32, (NREP * 16, 2 * NREP), 0)
    from_token = lax.broadcasted_iota(I32, (NREP * 16, 2 * NREP), 1) // NREP
    wanted = (line // 16) * SLOTS + ROWS + (line % 16) // 2
    route[...] = jnp.where((goal == wanted.astype(F32)) & (from_token == line % 2), 1.0, 0.0).astype(BF16)

    received(trec, 6)
    l_up.wait()
    low = trec[0]
    for n in range(1, TP):
        low = low + trec[n]
    low = low.astype(BF16).astype(F32)
    other = pltpu.roll(low, RANK, 1)
    spread = jnp.concatenate(
        [jnp.where(lane32 < RANK, low, other), jnp.where(lane32 < RANK, other, low)], axis=0
    )
    wide = jnp.where(chosen, jnp.concatenate([spread] * 8, axis=1), 0.0).astype(BF16)
    term = jnp.dot(wide, upv[...], preferred_element_type=F32)
    cs[:, 0, :] = term[:NREP]
    cs[:, 1, :] = term[NREP:]
    spread_out = jnp.dot(route[...], term.astype(BF16), preferred_element_type=F32)
    sb3[...] = spread_out.astype(BF16).reshape(NREP, 16, LANES)
    exchange((lambda d: cs.at[d], crec, 3))
    exchange((lambda d: sb3.at[d], mvrec, 5))

    received(grec, 4)
    received(wrec, 2)
    for n in range(ROWS):
        safe = jnp.clip(code_s[n], 0, 2 * NREP - 1)
        shift = (LANES - jnp.clip(line_s[n], 0, ROWS - 1) * 16) % LANES
        wq[2 * n : 2 * n + 2, :] = pltpu.roll(wrec[safe // 2], shift, 1)
    column = wq[...].T[0:16, :] * 0.5
    for n in range(ROWS):
        safe = jnp.clip(code_s[n], 0, 2 * NREP - 1)
        base[n] = jnp.where(code_s[n] >= 0, grec[safe // 2, safe % 2].astype(F32), 0.0)
        gain0[n] = jnp.broadcast_to(column[:, 2 * n : 2 * n + 1], (16, LANES))
        gain1[n] = jnp.broadcast_to(column[:, 2 * n + 1 : 2 * n + 2], (16, LANES))
    received(crec, 3)
    for r in range(ROWS):
        back = crec[owners[r]]
        value0 = (pvs[r : r + 1, :] + 0.5 * back[0:1]).astype(BF16).astype(F32)
        value1 = (pvs[ROWS + r : ROWS + r + 1, :] + 0.5 * back[1:2]).astype(BF16).astype(F32)
        done = (mixed[r] + wn0s[r] * value0 + wn1s[r] * value1).astype(BF16)
        kept = slots[r] == me * SLOTS + r
        out[r] = jnp.where(kept, done, jnp.zeros((16, LANES), BF16))
    received(mvrec, 5)
    extra = mvrec[0].astype(F32)
    for n in range(1, NREP):
        extra = extra + mvrec[n].astype(F32)
    for n in range(ROWS):
        added = gain0[n] * extra[2 * n : 2 * n + 1] + gain1[n] * extra[2 * n + 1 : 2 * n + 2]
        out[ROWS + n] = (base[n] + added).astype(BF16)

    def sent(ref, n):
        pltpu.make_async_copy(ref, ref, send_sem.at[n]).wait()

    sent(sb.at[pl.ds(0, NREP - 1)], 0)
    sent(mrec.at[pl.ds(0, NREP - 1)], 1)
    sent(trec.at[pl.ds(0, TP - 1)], 6)
    sent(wrec.at[pl.ds(0, NREP - 1)], 2)
    sent(cs.at[pl.ds(0, NREP - 1)], 3)
    sent(sb4.at[pl.ds(0, NREP - 1)], 4)
    sent(sb3.at[pl.ds(0, NREP - 1)], 5)


def shards(hidden, queries, wk, wv, down, up, ridx, home, table, lengths, serve, kc, vc):
    hid = hidden.reshape(ROWS, 2, CHUNKS, LANES).transpose(0, 2, 1, 3).reshape(ROWS, LANES, LANES)
    qin = queries.reshape(ROWS, 2, 8, LANES).transpose(0, 2, 1, 3).reshape(ROWS, 16, LANES)
    dn = jnp.swapaxes(down, 1, 2)
    upr = up.reshape(ADP * RANK, LANES)
    vmem, smem = pltpu.VMEM, pltpu.SMEM
    scratch = [
        vmem((ROWS, LANES, LANES), BF16), vmem((ROWS, 16, LANES), BF16), vmem((8192, LANES), BF16), vmem((8192, LANES), BF16),
        vmem((ADP, RANK, 1024), BF16), vmem((ADP * RANK, LANES), BF16), vmem((64, LANES, LANES), BF16), vmem((64, LANES, LANES), BF16),
        smem((8,), I32), smem((512,), I32), smem((8, 8), I32), smem((1, 8), I32), smem((8,), I32),
        vmem((ROWS * LANES, LANES), F32), vmem((16, 8192), BF16),
        vmem((NREP, 16, LANES), BF16), vmem((NREP, 16, LANES), BF16),
        vmem((NREP * 16, LANES), F32), vmem((2 * NREP, 1024), BF16),
        vmem((1, LANES), I32), vmem((NREP, 1, LANES), I32),
        vmem((NREP, LANES), F32), vmem((TP, NREP, LANES), F32),
        vmem((NREP, 2, LANES), F32), vmem((NREP, 2, LANES), F32),
        vmem((ROWS, 16, LANES), F32), vmem((ROWS, 16, LANES), F32), vmem((ROWS, 16, LANES), F32),
        vmem((16, LANES), F32), vmem((16, LANES), F32),
        vmem((ROWS, 16, LANES), BF16), vmem((ROWS, 16, LANES), F32), vmem((2, LANES), F32), vmem((NREP, 2, LANES), F32),
        vmem((NREP, 2, 16, LANES), BF16), vmem((NREP, 2, 16, LANES), BF16),
        vmem((NREP * 16, 2 * NREP), BF16), vmem((NREP, 16, LANES), BF16), vmem((NREP, 16, LANES), BF16),
        vmem((ROWS, 16, LANES), F32), vmem((ROWS, 16, LANES), F32), vmem((ROWS, 16, LANES), F32),
        vmem((8, LANES), I32), smem((8, LANES), I32), smem((ROWS,), I32), smem((ROWS,), I32), vmem((16, LANES), F32),
        pltpu.SemaphoreType.DMA((14,)), pltpu.SemaphoreType.DMA((7,)), pltpu.SemaphoreType.DMA((7,)),
    ]
    hid, qin, wk, wv, dn, upr, ridx, home, table, lengths, serve, kc, vc = (pltpu.with_memory_space_constraint(a, pltpu.HBM) for a in (hid, qin, wk, wv, dn, upr, ridx, home, table, lengths, serve, kc, vc))
    result = pl.pallas_call(
        kernel,
        out_shape=jax.ShapeDtypeStruct((SLOTS, 16, LANES), BF16),
        in_specs=[pl.BlockSpec(memory_space=pltpu.HBM)] * 13,
        out_specs=pl.BlockSpec(memory_space=pltpu.VMEM),
        scratch_shapes=scratch,
        compiler_params=pltpu.CompilerParams(
            collective_id=0, has_side_effects=True, vmem_limit_bytes=48 << 20
        ),
        name="decode",
    )(hid, qin, wk, wv, dn, upr, ridx, home, table, lengths, serve, kc, vc)
    return result.reshape(SLOTS, 8, 2, LANES).transpose(0, 2, 1, 3).reshape(SLOTS, 2, 1024)


def solution(mesh):
    placed = (
        P("rep", None, None),
        P("rep", None, "tp"),
        P(None, "tp"),
        P(None, "tp"),
        P("rep", "tp", None),
        P("rep", None, "tp"),
        P("rep"),
        P(),
        P("rep", None),
        P("rep", None),
        P("rep"),
        P("rep", None, "tp"),
        P("rep", None, "tp"),
    )
    return jax.shard_map(
        shards, mesh=mesh, in_specs=placed, out_specs=P("rep", None, "tp"), check_vma=False
    )
```

```python
import functools
import math

import jax
import jax.numpy as jnp
from jax import lax
from jax.experimental import pallas as pl
from jax.experimental.pallas import tpu as pltpu
from jax.sharding import PartitionSpec as P

MESH = pl.DeviceIdType.MESH
F32, BF16, I32 = jnp.float32, jnp.bfloat16, jnp.int32

NX, NZ, TP = 4, 8, 8
NREP = NX * NZ
ROWS, SLOTS, ADP, RANK = 8, 16, 16, 64
LANES = 128
CHUNKS = 64
NT = (((1,), (1,)), ((), ()))
LOG_BASE = math.log(1000000.0)
FAR_FIRST = sorted(
    [(x, z) for x in range(NX) for z in range(NZ) if x or z],
    key=lambda o: -(min(o[0], NX - o[0]) + min(o[1], NZ - o[1])),
)


def kernel(
    hid, qin, wk, wv, dn, up, ridx, home, table, length, serve, kc, vc,
    out,
    hidv, qv, wkv, wvv, dnv, upv, kv, vv, ridx_s, home_s, table_s, length_s, serve_s,
    hf, xl, sb, arr, af, ai, xs, mb, mrec, tb, trec, mixed, wn0s, wn1s, nkf, pvs, plain, gains, sb4, grec,
    route, sb3, mvrec, base, gain0, gain1, tab, tab_s, code_s, line_s, wq, in_sem, send_sem, recv_sem,
):
    me = lax.axis_index("rep")
    tp = lax.axis_index("tp")
    mx, mz = me // NZ, me % NZ

    to_x = [((mx + n) % NX) * NZ for n in range(NX)]
    to_z = [(mz + n) % NZ for n in range(NZ)]

    def peers(do):
        for dx, dz in FAR_FIRST:
            do(to_x[dx] + to_z[dz])

    def tp_peers(do):
        for a in (4, 5, 3, 2, 6, 1, 7):
            do((tp + a) % TP)

    bar = pltpu.get_barrier_semaphore()
    peers(lambda d: pl.semaphore_signal(bar, inc=1, device_id=(d, tp), device_id_type=MESH))
    tp_peers(lambda d: pl.semaphore_signal(bar, inc=1, device_id=(me, d), device_id_type=MESH))

    pairs = [
        (ridx, ridx_s), (home, home_s), (serve, serve_s), (hid, hidv), (length, length_s), (table, table_s),
        (wk, wkv), (wv, wvv), (qin, qv), (kc, kv), (vc, vv), (dn, dnv), (up, upv),
    ]
    loads = [pltpu.make_async_copy(s, d, in_sem.at[n]) for n, (s, d) in enumerate(pairs)]
    for c in loads:
        c.start()
    (l_ridx, l_home, l_serve, l_hid, l_len, l_tab, l_wk, l_wv, l_q, l_k, l_v, l_dn, l_up) = loads

    l_hid.wait()
    hf[...] = hidv[...].reshape(ROWS * LANES, LANES).astype(F32)
    for c in range(CHUNKS):
        both = [hf[pl.ds(2 * c + t, ROWS, stride=LANES), :] for t in range(2)]
        xl[:, c * LANES : (c + 1) * LANES] = jnp.concatenate(both, axis=0).astype(BF16)
    l_ridx.wait()
    l_home.wait()
    l_serve.wait()
    homes = [home_s[ridx_s[i]] for i in range(ROWS)]
    owners = [h // ADP for h in homes]
    slots = [serve_s[i] for i in range(ROWS)]
    lane1 = lax.broadcasted_iota(I32, (1, LANES), 1)
    meta = jnp.zeros((1, LANES), I32)
    for i in range(ROWS):
        for n, value in enumerate((owners[i], slots[i] // SLOTS, homes[i] % ADP, slots[i] % SLOTS)):
            meta = jnp.where(lane1 == n * ROWS + i, value, meta)
    line = jnp.full((1, LANES), -1, I32)
    for i in range(ROWS):
        line = jnp.where(lane1 == i, slots[i], line)
    mb[...] = line
    meta = jnp.broadcast_to(meta.astype(F32), (16, LANES)).astype(BF16)
    mine = pl.multiple_of(tp * 16, 16)

    targets = [s // SLOTS for s in slots]
    none = jnp.zeros((1, LANES), I32)
    to_home, first, second, count = none, none, none, none
    for i in range(ROWS):
        to_home = jnp.where(lane1 == owners[i], i, to_home)
        here = lane1 == targets[i]
        first = jnp.where(here & (count == 0), i, first)
        second = jnp.where(here & (count == 1), i, second)
        count = count + here.astype(I32)
    tab[...] = jnp.zeros((8, LANES), I32)
    tab[0:1, :] = to_home
    tab[1:2, :] = first
    tab[2:3, :] = second
    to_smem = pltpu.make_async_copy(tab, tab_s, in_sem.at[13])
    to_smem.start()
    l_wk.wait()
    new_keys = jnp.dot(xl[...], wkv[...], preferred_element_type=F32)
    l_len.wait()
    row16 = lax.broadcasted_iota(I32, (2 * ROWS, LANES), 0)
    lane16 = lax.broadcasted_iota(I32, (2 * ROWS, LANES), 1)
    position = jnp.zeros((2 * ROWS, LANES), I32)
    for i in range(ROWS):
        for t in range(2):
            position = jnp.where(row16 == t * ROWS + i, length_s[0, i] + t, position)
    half = (lane16 % (LANES // 2)).astype(F32)
    angle = position.astype(F32) * jnp.exp(half * (-2.0 * LOG_BASE / LANES))
    turned = pltpu.roll(new_keys, LANES // 2, 1)
    sine = jnp.where(lane16 < LANES // 2, -jnp.sin(angle), jnp.sin(angle))
    nkf[...] = (new_keys * jnp.cos(angle) + turned * sine).astype(BF16).astype(F32)
    l_wv.wait()
    pvs[...] = jnp.dot(xl[...], wvv[...], preferred_element_type=F32)

    to_smem.wait()

    def fill(d, carry):
        sb[d, 0:16] = hidv[tab_s[0, d], pl.ds(mine, 16), :]
        sb[d, 16:32] = meta
        return carry

    lax.fori_loop(0, NREP, fill, 0)

    pl.semaphore_wait(bar, NREP - 1 + TP - 1)

    def exchange(src, dst, lines, n):
        part = pl.ds(0, lines)

        def one(d):
            pltpu.make_async_remote_copy(
                src.at[d, part], dst.at[me, part], send_sem.at[n], recv_sem.at[n], device_id=(d, tp), device_id_type=MESH
            ).start()

        peers(one)
        pltpu.make_async_copy(src.at[me, part], dst.at[me, part], recv_sem.at[n]).start()

    def received(dst, lines, n):
        every = dst.at[:, pl.ds(0, lines)]
        pltpu.make_async_copy(every, every, recv_sem.at[n]).wait()

    exchange(sb, arr, 18, 0)

    def tell(d):
        pltpu.make_async_remote_copy(
            mb, mrec.at[me], send_sem.at[4], recv_sem.at[4], device_id=(d, tp), device_id_type=MESH
        ).start()

    peers(tell)
    pltpu.make_async_copy(mb, mrec.at[me], recv_sem.at[4]).start()

    l_tab.wait()
    l_q.wait()
    l_k.wait()
    l_v.wait()
    scale = LANES ** (-0.5)
    span = ROWS * LANES
    token = lax.broadcasted_iota(I32, (16, 1), 0) % 2
    place = lax.broadcasted_iota(I32, (16, span), 1)

    def attend(r, carry):
        q = qv[r]
        pages = [table_s[r, n] for n in range(8)]
        keys = jnp.concatenate([kv[p] for p in pages], axis=0)
        old = lax.dot_general(q, keys, NT, preferred_element_type=F32) * scale
        old = jnp.where(place < length_s[0, r], old, -jnp.inf)
        qf = q.astype(F32)
        new0 = jnp.sum(qf * nkf[pl.ds(r, 1), :], axis=-1, keepdims=True) * scale
        new1 = jnp.sum(qf * nkf[pl.ds(ROWS + r, 1), :], axis=-1, keepdims=True) * scale
        new1 = jnp.where(token == 1, new1, -jnp.inf)
        peak = jnp.maximum(jnp.max(old, axis=-1, keepdims=True), jnp.maximum(new0, new1))
        eo, e0, e1 = jnp.exp(old - peak), jnp.exp(new0 - peak), jnp.exp(new1 - peak)
        total = jnp.sum(eo, axis=-1, keepdims=True) + e0 + e1
        weights = (eo / total).astype(BF16)
        values = jnp.concatenate([vv[p] for p in pages], axis=0)
        mixed[r] = jnp.dot(weights, values, preferred_element_type=F32)
        w0 = jnp.broadcast_to((e0 / total).astype(BF16).astype(F32), (16, LANES))
        w1 = jnp.broadcast_to((e1 / total).astype(BF16).astype(F32), (16, LANES))
        wn0s[r] = w0
        wn1s[r] = w1
        fresh = w0 * pvs[pl.ds(r, 1), :] + w1 * pvs[pl.ds(ROWS + r, 1), :]
        plain[r] = (mixed[r] + fresh).astype(BF16)
        gains[r] = jnp.where(lane16 == 0, w0, w1)
        return carry

    def several(n, carry):
        for u in range(4):
            attend(n * 4 + u, carry)
        return carry

    lax.fori_loop(0, ROWS // 4, several, 0)

    gain_lines = gains[...].reshape(ROWS * 16, LANES).T[0:16, :].astype(BF16)

    def moved(d, carry):
        one, two = tab_s[1, d], tab_s[2, d]
        sb4[d, 0:16] = plain[one]
        sb4[d, 16:32] = plain[two]
        sb4[d, 32:48] = gain_lines
        return carry

    lax.fori_loop(0, NREP, moved, 0)
    exchange(sb4, grec, 34, 1)

    l_dn.wait()
    l_up.wait()
    received(arr, 18, 0)
    af[...] = arr[:, 0:16, :].reshape(NREP * 16, LANES).astype(F32)
    ai[...] = arr[:, 16:32, :].reshape(NREP * 16, LANES).astype(F32)
    for c in range(8):
        for t in range(2):
            piece = af[pl.ds(2 * c + t, NREP, stride=16), :]
            xs[t * NREP : (t + 1) * NREP, c * LANES : (c + 1) * LANES] = piece.astype(BF16)
    every = lax.dot_general(xs[...], dnv[...].reshape(ADP * RANK, 8 * LANES), NT, preferred_element_type=F32)
    known = ai[pl.ds(0, NREP, stride=16), :].astype(I32)
    lane32 = lax.broadcasted_iota(I32, (NREP, LANES), 1)
    own = ((known == me) & (lane32 < ROWS)).astype(I32)
    within = jnp.where(pltpu.roll(own, 2 * ROWS, 1) > 0, known, 0)
    within = jnp.sum(within.astype(F32), axis=-1, keepdims=True).astype(I32)
    pick = jnp.concatenate([within, within], axis=0)
    block = lax.broadcasted_iota(I32, (2 * NREP, ADP * RANK), 1) // RANK
    chosen = block == pick
    every = jnp.where(chosen, every, 0.0)
    folded = every[:, :LANES]
    for v in range(1, 8):
        folded = folded + every[:, v * LANES : (v + 1) * LANES]
    folded = folded + pltpu.roll(folded, RANK, 1)
    tb[...] = jnp.where(lane32 < RANK, folded[:NREP], folded[NREP:])

    def to_tp(d):
        pltpu.make_async_remote_copy(
            tb, trec.at[tp], send_sem.at[2], recv_sem.at[2], device_id=(me, d), device_id_type=MESH
        ).start()

    tp_peers(to_tp)
    pltpu.make_async_copy(tb, trec.at[tp], recv_sem.at[2]).start()

    pltpu.make_async_copy(mrec, mrec, recv_sem.at[4]).wait()
    named = mrec[:, 0, :]
    target = named // SLOTS
    rank = jnp.zeros((NREP, LANES), I32)
    for back in range(1, ROWS):
        same = (pltpu.roll(target, back, 1) == target) & (lane32 >= back)
        rank = rank + same.astype(I32)
    code = lax.broadcasted_iota(I32, (NREP, LANES), 0) * 2 + rank
    for n in range(ROWS):
        hit = (lane32 < ROWS) & (named == me * SLOTS + ROWS + n)
        code_s[n] = jnp.max(jnp.where(hit, code, -1))
        line_s[n] = jnp.max(jnp.where(hit, lane32, 0))

    slot = known * SLOTS + pltpu.roll(known, LANES - 2 * ROWS, 1)
    goal = jnp.sum(jnp.where(pltpu.roll(own, ROWS, 1) > 0, slot, 0).astype(F32), axis=-1, keepdims=True)
    held = jnp.sum(own.astype(F32), axis=-1, keepdims=True)
    goal = jnp.where(held > 0.0, goal, -1.0)
    goal = jnp.broadcast_to(jnp.concatenate([goal, goal], axis=0), (2 * NREP, LANES)).T[0:1, :]
    line = lax.broadcasted_iota(I32, (NREP * 32, 2 * NREP), 0)
    column = lax.broadcasted_iota(I32, (NREP * 32, 2 * NREP), 1)
    to, part = line // 32, line % 32
    for_slot = (part < 16) & (goal == (to * SLOTS + ROWS + part // 2).astype(F32))
    for_own = (part >= 16) & (part < 18) & (column % NREP == to)
    wanted = (for_slot | for_own) & (column // NREP == part % 2)
    route[...] = jnp.where(wanted, 1.0, 0.0).astype(BF16)

    pltpu.make_async_copy(trec, trec, recv_sem.at[2]).wait()
    low = trec[0]
    for n in range(1, TP):
        low = low + trec[n]
    low = low.astype(BF16).astype(F32)
    other = pltpu.roll(low, RANK, 1)
    spread = jnp.concatenate(
        [jnp.where(lane32 < RANK, low, other), jnp.where(lane32 < RANK, other, low)], axis=0
    )
    wide = jnp.where(chosen, jnp.concatenate([spread] * 8, axis=1), 0.0).astype(BF16)
    term = jnp.dot(wide, upv[...], preferred_element_type=F32)
    sb3[...] = jnp.dot(route[...], term.astype(BF16), preferred_element_type=F32).astype(BF16).reshape(NREP, 32, LANES)
    exchange(sb3, mvrec, 18, 3)

    received(grec, 34, 1)
    for n in range(ROWS):
        safe = jnp.clip(code_s[n], 0, 2 * NREP - 1)
        shift = (LANES - jnp.clip(line_s[n], 0, ROWS - 1) * 16) % LANES
        wq[2 * n : 2 * n + 2, :] = pltpu.roll(grec[safe // 2, 32:48].astype(F32), shift, 1)[0:2]
    column = wq[...].T[0:16, :] * 0.5
    for n in range(ROWS):
        safe = jnp.clip(code_s[n], 0, 2 * NREP - 1)
        one, two = grec[safe // 2, 0:16].astype(F32), grec[safe // 2, 16:32].astype(F32)
        base[n] = jnp.where(code_s[n] >= 0, jnp.where(safe % 2 == 1, two, one), 0.0)
        gain0[n] = jnp.broadcast_to(column[:, 2 * n : 2 * n + 1], (16, LANES))
        gain1[n] = jnp.broadcast_to(column[:, 2 * n + 1 : 2 * n + 2], (16, LANES))
    received(mvrec, 18, 3)
    for r in range(ROWS):
        back = mvrec[owners[r], 16:32].astype(F32)
        value0 = (pvs[r : r + 1, :] + 0.5 * back[0:1]).astype(BF16).astype(F32)
        value1 = (pvs[ROWS + r : ROWS + r + 1, :] + 0.5 * back[1:2]).astype(BF16).astype(F32)
        done = (mixed[r] + wn0s[r] * value0 + wn1s[r] * value1).astype(BF16)
        kept = slots[r] == me * SLOTS + r
        out[r] = jnp.where(kept, done, jnp.zeros((16, LANES), BF16))
    extra = mvrec[0, 0:16].astype(F32)
    for n in range(1, NREP):
        extra = extra + mvrec[n, 0:16].astype(F32)
    for n in range(ROWS):
        added = gain0[n] * extra[2 * n : 2 * n + 1] + gain1[n] * extra[2 * n + 1 : 2 * n + 2]
        out[ROWS + n] = (base[n] + added).astype(BF16)

    def sent(ref, n):
        pltpu.make_async_copy(ref, ref, send_sem.at[n]).wait()

    others = pl.ds(0, NREP - 1)
    sent(sb.at[others, pl.ds(0, 18)], 0)
    sent(mrec.at[others], 4)
    sent(sb4.at[others, pl.ds(0, 34)], 1)
    sent(trec.at[pl.ds(0, TP - 1)], 2)
    sent(sb3.at[others, pl.ds(0, 18)], 3)


def shards(hidden, queries, wk, wv, down, up, ridx, home, table, lengths, serve, kc, vc):
    hid = hidden.reshape(ROWS, 2, CHUNKS, LANES).transpose(0, 2, 1, 3).reshape(ROWS, LANES, LANES)
    qin = queries.reshape(ROWS, 2, 8, LANES).transpose(0, 2, 1, 3).reshape(ROWS, 16, LANES)
    dn = jnp.swapaxes(down, 1, 2)
    upr = up.reshape(ADP * RANK, LANES)
    vmem, smem = pltpu.VMEM, pltpu.SMEM
    scratch = [
        vmem((ROWS, LANES, LANES), BF16), vmem((ROWS, 16, LANES), BF16), vmem((8192, LANES), BF16), vmem((8192, LANES), BF16),
        vmem((ADP, RANK, 1024), BF16), vmem((ADP * RANK, LANES), BF16), vmem((64, LANES, LANES), BF16), vmem((64, LANES, LANES), BF16),
        smem((8,), I32), smem((512,), I32), smem((8, 8), I32), smem((1, 8), I32), smem((8,), I32),
        vmem((ROWS * LANES, LANES), F32), vmem((16, 8192), BF16),
        vmem((NREP, 32, LANES), BF16), vmem((NREP, 32, LANES), BF16),
        vmem((NREP * 16, LANES), F32), vmem((NREP * 16, LANES), F32), vmem((2 * NREP, 1024), BF16),
        vmem((1, LANES), I32), vmem((NREP, 1, LANES), I32),
        vmem((NREP, LANES), F32), vmem((TP, NREP, LANES), F32),
        vmem((ROWS, 16, LANES), F32), vmem((ROWS, 16, LANES), F32), vmem((ROWS, 16, LANES), F32),
        vmem((16, LANES), F32), vmem((16, LANES), F32),
        vmem((ROWS, 16, LANES), BF16), vmem((ROWS, 16, LANES), F32),
        vmem((NREP, 48, LANES), BF16), vmem((NREP, 48, LANES), BF16),
        vmem((NREP * 32, 2 * NREP), BF16), vmem((NREP, 32, LANES), BF16), vmem((NREP, 32, LANES), BF16),
        vmem((ROWS, 16, LANES), F32), vmem((ROWS, 16, LANES), F32), vmem((ROWS, 16, LANES), F32),
        vmem((8, LANES), I32), smem((8, LANES), I32), smem((ROWS,), I32), smem((ROWS,), I32), vmem((16, LANES), F32),
        pltpu.SemaphoreType.DMA((14,)), pltpu.SemaphoreType.DMA((5,)), pltpu.SemaphoreType.DMA((5,)),
    ]
    hid, qin, wk, wv, dn, upr, ridx, home, table, lengths, serve, kc, vc = (pltpu.with_memory_space_constraint(a, pltpu.HBM) for a in (hid, qin, wk, wv, dn, upr, ridx, home, table, lengths, serve, kc, vc))
    result = pl.pallas_call(
        kernel,
        out_shape=jax.ShapeDtypeStruct((SLOTS, 16, LANES), BF16),
        in_specs=[pl.BlockSpec(memory_space=pltpu.HBM)] * 13,
        out_specs=pl.BlockSpec(memory_space=pltpu.VMEM),
        scratch_shapes=scratch,
        compiler_params=pltpu.CompilerParams(
            collective_id=0, has_side_effects=True, vmem_limit_bytes=48 << 20
        ),
        name="decode",
    )(hid, qin, wk, wv, dn, upr, ridx, home, table, lengths, serve, kc, vc)
    return result.reshape(SLOTS, 8, 2, LANES).transpose(0, 2, 1, 3).reshape(SLOTS, 2, 1024)


def solution(mesh):
    placed = (
        P("rep", None, None),
        P("rep", None, "tp"),
        P(None, "tp"),
        P(None, "tp"),
        P("rep", "tp", None),
        P("rep", None, "tp"),
        P("rep"),
        P(),
        P("rep", None),
        P("rep", None),
        P("rep"),
        P("rep", None, "tp"),
        P("rep", None, "tp"),
    )
    return jax.shard_map(
        shards, mesh=mesh, in_specs=placed, out_specs=P("rep", None, "tp"), check_vma=False
    )
```

```python
import functools
import math

import jax
import jax.numpy as jnp
from jax import lax
from jax.experimental import pallas as pl
from jax.experimental.pallas import tpu as pltpu
from jax.sharding import PartitionSpec as P

MESH = pl.DeviceIdType.MESH
F32, BF16, I32 = jnp.float32, jnp.bfloat16, jnp.int32

NX, NZ, TP = 4, 8, 8
NREP = NX * NZ
ROWS, SLOTS, ADP, RANK = 8, 16, 16, 64
LANES = 128
CHUNKS = 64
NT = (((1,), (1,)), ((), ()))
LOG_BASE = math.log(1000000.0)
FAR_FIRST = sorted(
    [(x, z) for x in range(NX) for z in range(NZ) if x or z],
    key=lambda o: -(min(o[0], NX - o[0]) + min(o[1], NZ - o[1])),
)


def kernel(
    hid, qin, wk, wv, dn, up, ridx, home, table, length, serve, kc, vc,
    out,
    hidv, qv, wkv, wvv, dnv, upv, kv, vv, ridx_s, home_s, table_s, length_s, serve_s,
    hf, xl, sb, arr, af, ai, xs, mb, mrec, tb, trec, mixed, wn0s, wn1s, nkf, pvs, plain, gains, sb4, grec,
    route, sb3, mvrec, base, gain0, gain1, tab, tab_s, code_s, line_s, wq, in_sem, send_sem, recv_sem,
):
    me = lax.axis_index("rep")
    tp = lax.axis_index("tp")
    mx, mz = me // NZ, me % NZ

    to_x = [((mx + n) % NX) * NZ for n in range(NX)]
    to_z = [(mz + n) % NZ for n in range(NZ)]

    def peers(do):
        for dx, dz in FAR_FIRST:
            do(to_x[dx] + to_z[dz])

    def tp_peers(do):
        for a in (4, 5, 3, 2, 6, 1, 7):
            do((tp + a) % TP)

    bar = pltpu.get_barrier_semaphore()
    peers(lambda d: pl.semaphore_signal(bar, inc=1, device_id=(d, tp), device_id_type=MESH))
    tp_peers(lambda d: pl.semaphore_signal(bar, inc=1, device_id=(me, d), device_id_type=MESH))

    pairs = [
        (ridx, ridx_s), (home, home_s), (serve, serve_s), (hid, hidv), (length, length_s), (table, table_s),
        (wk, wkv), (wv, wvv), (qin, qv), (kc, kv), (vc, vv), (dn, dnv), (up, upv),
    ]
    loads = [pltpu.make_async_copy(s, d, in_sem.at[n]) for n, (s, d) in enumerate(pairs)]
    for c in loads:
        c.start()
    (l_ridx, l_home, l_serve, l_hid, l_len, l_tab, l_wk, l_wv, l_q, l_k, l_v, l_dn, l_up) = loads

    l_hid.wait()
    hf[...] = hidv[...].reshape(ROWS * LANES, LANES).astype(F32)
    for c in range(CHUNKS):
        both = [hf[pl.ds(2 * c + t, ROWS, stride=LANES), :] for t in range(2)]
        xl[:, c * LANES : (c + 1) * LANES] = jnp.concatenate(both, axis=0).astype(BF16)
    l_ridx.wait()
    l_home.wait()
    l_serve.wait()
    homes = [home_s[ridx_s[i]] for i in range(ROWS)]
    owners = [h // ADP for h in homes]
    slots = [serve_s[i] for i in range(ROWS)]
    lane1 = lax.broadcasted_iota(I32, (1, LANES), 1)
    meta = jnp.zeros((1, LANES), I32)
    for i in range(ROWS):
        for n, value in enumerate((owners[i], slots[i] // SLOTS, homes[i] % ADP, slots[i] % SLOTS)):
            meta = jnp.where(lane1 == n * ROWS + i, value, meta)
    line = jnp.full((1, LANES), -1, I32)
    for i in range(ROWS):
        line = jnp.where(lane1 == i, slots[i], line)
    mb[...] = line
    meta = jnp.broadcast_to(meta.astype(F32), (16, LANES)).astype(BF16)
    mine = pl.multiple_of(tp * 16, 16)

    targets = [s // SLOTS for s in slots]
    none = jnp.zeros((1, LANES), I32)
    to_home, first, second, count = none, none, none, none
    for i in range(ROWS):
        to_home = jnp.where(lane1 == owners[i], i, to_home)
        here = lane1 == targets[i]
        first = jnp.where(here & (count == 0), i, first)
        second = jnp.where(here & (count == 1), i, second)
        count = count + here.astype(I32)
    tab[...] = jnp.zeros((8, LANES), I32)
    tab[0:1, :] = to_home
    tab[1:2, :] = first
    tab[2:3, :] = second
    to_smem = pltpu.make_async_copy(tab, tab_s, in_sem.at[13])
    to_smem.start()
    l_wk.wait()
    new_keys = jnp.dot(xl[...], wkv[...], preferred_element_type=F32)
    l_len.wait()
    row16 = lax.broadcasted_iota(I32, (2 * ROWS, LANES), 0)
    lane16 = lax.broadcasted_iota(I32, (2 * ROWS, LANES), 1)
    position = jnp.zeros((2 * ROWS, LANES), I32)
    for i in range(ROWS):
        for t in range(2):
            position = jnp.where(row16 == t * ROWS + i, length_s[0, i] + t, position)
    half = (lane16 % (LANES // 2)).astype(F32)
    angle = position.astype(F32) * jnp.exp(half * (-2.0 * LOG_BASE / LANES))
    turned = pltpu.roll(new_keys, LANES // 2, 1)
    sine = jnp.where(lane16 < LANES // 2, -jnp.sin(angle), jnp.sin(angle))
    nkf[...] = (new_keys * jnp.cos(angle) + turned * sine).astype(BF16).astype(F32)
    l_wv.wait()
    pvs[...] = jnp.dot(xl[...], wvv[...], preferred_element_type=F32)

    to_smem.wait()

    def fill(d, carry):
        sb[d, 0:16] = hidv[tab_s[0, d], pl.ds(mine, 16), :]
        sb[d, 16:32] = meta
        return carry

    lax.fori_loop(0, NREP, fill, 0)

    pl.semaphore_wait(bar, NREP - 1 + TP - 1)

    def exchange(src, dst, lines, n):
        part = pl.ds(0, lines)

        def one(d):
            pltpu.make_async_remote_copy(
                src.at[d, part], dst.at[me, part], send_sem.at[n], recv_sem.at[n], device_id=(d, tp), device_id_type=MESH
            ).start()

        peers(one)
        pltpu.make_async_copy(src.at[me, part], dst.at[me, part], recv_sem.at[n]).start()

    def received(dst, lines, n):
        every = dst.at[:, pl.ds(0, lines)]
        pltpu.make_async_copy(every, every, recv_sem.at[n]).wait()

    exchange(sb, arr, 18, 0)

    def tell(d):
        pltpu.make_async_remote_copy(
            mb, mrec.at[me], send_sem.at[4], recv_sem.at[4], device_id=(d, tp), device_id_type=MESH
        ).start()

    peers(tell)
    pltpu.make_async_copy(mb, mrec.at[me], recv_sem.at[4]).start()

    l_tab.wait()
    l_q.wait()
    l_k.wait()
    l_v.wait()
    scale = LANES ** (-0.5)
    span = ROWS * LANES
    token = lax.broadcasted_iota(I32, (16, 1), 0) % 2
    place = lax.broadcasted_iota(I32, (16, span), 1)

    def attend(r, carry):
        q = qv[r]
        pages = [table_s[r, n] for n in range(8)]
        keys = jnp.concatenate([kv[p] for p in pages], axis=0)
        old = lax.dot_general(q, keys, NT, preferred_element_type=F32) * scale
        old = jnp.where(place < length_s[0, r], old, -jnp.inf)
        qf = q.astype(F32)
        new0 = jnp.sum(qf * nkf[pl.ds(r, 1), :], axis=-1, keepdims=True) * scale
        new1 = jnp.sum(qf * nkf[pl.ds(ROWS + r, 1), :], axis=-1, keepdims=True) * scale
        new1 = jnp.where(token == 1, new1, -jnp.inf)
        peak = jnp.maximum(jnp.max(old, axis=-1, keepdims=True), jnp.maximum(new0, new1))
        eo, e0, e1 = jnp.exp(old - peak), jnp.exp(new0 - peak), jnp.exp(new1 - peak)
        total = jnp.sum(eo, axis=-1, keepdims=True) + e0 + e1
        weights = (eo / total).astype(BF16)
        values = jnp.concatenate([vv[p] for p in pages], axis=0)
        mixed[r] = jnp.dot(weights, values, preferred_element_type=F32)
        w0 = jnp.broadcast_to((e0 / total).astype(BF16).astype(F32), (16, LANES))
        w1 = jnp.broadcast_to((e1 / total).astype(BF16).astype(F32), (16, LANES))
        wn0s[r] = w0
        wn1s[r] = w1
        fresh = w0 * pvs[pl.ds(r, 1), :] + w1 * pvs[pl.ds(ROWS + r, 1), :]
        plain[r] = (mixed[r] + fresh).astype(BF16)
        gains[r] = jnp.where(lane16 == 0, w0, w1)
        return carry

    def several(n, carry):
        for u in range(4):
            attend(n * 4 + u, carry)
        return carry

    lax.fori_loop(0, ROWS // 4, several, 0)

    gain_lines = gains[...].reshape(ROWS * 16, LANES).T[0:16, :].astype(BF16)

    def moved(d, carry):
        one, two = tab_s[1, d], tab_s[2, d]
        sb4[d, 0:16] = plain[one]
        sb4[d, 16:32] = plain[two]
        sb4[d, 32:48] = gain_lines
        return carry

    lax.fori_loop(0, NREP, moved, 0)
    exchange(sb4, grec, 34, 1)

    l_dn.wait()
    l_up.wait()
    received(arr, 18, 0)
    af[...] = arr[:, 0:16, :].reshape(NREP * 16, LANES).astype(F32)
    ai[...] = arr[:, 16:32, :].reshape(NREP * 16, LANES).astype(F32)
    for c in range(8):
        for t in range(2):
            piece = af[pl.ds(2 * c + t, NREP, stride=16), :]
            xs[t * NREP : (t + 1) * NREP, c * LANES : (c + 1) * LANES] = piece.astype(BF16)
    every = lax.dot_general(xs[...], dnv[...].reshape(ADP * RANK, 8 * LANES), NT, preferred_element_type=F32)
    known = ai[pl.ds(0, NREP, stride=16), :].astype(I32)
    lane32 = lax.broadcasted_iota(I32, (NREP, LANES), 1)
    own = ((known == me) & (lane32 < ROWS)).astype(I32)
    within = jnp.where(pltpu.roll(own, 2 * ROWS, 1) > 0, known, 0)
    within = jnp.sum(within.astype(F32), axis=-1, keepdims=True).astype(I32)
    pick = jnp.concatenate([within, within], axis=0)
    block = lax.broadcasted_iota(I32, (2 * NREP, ADP * RANK), 1) // RANK
    chosen = block == pick
    every = jnp.where(chosen, every, 0.0)
    folded = every[:, :LANES]
    for v in range(1, 8):
        folded = folded + every[:, v * LANES : (v + 1) * LANES]
    folded = folded + pltpu.roll(folded, RANK, 1)
    tb[...] = jnp.where(lane32 < RANK, folded[:NREP], folded[NREP:])

    def to_tp(d):
        pltpu.make_async_remote_copy(
            tb, trec.at[tp], send_sem.at[2], recv_sem.at[2], device_id=(me, d), device_id_type=MESH
        ).start()

    tp_peers(to_tp)
    pltpu.make_async_copy(tb, trec.at[tp], recv_sem.at[2]).start()

    pltpu.make_async_copy(mrec, mrec, recv_sem.at[4]).wait()
    named = mrec[:, 0, :]
    target = named // SLOTS
    rank = jnp.zeros((NREP, LANES), I32)
    for back in range(1, ROWS):
        same = (pltpu.roll(target, back, 1) == target) & (lane32 >= back)
        rank = rank + same.astype(I32)
    code = lax.broadcasted_iota(I32, (NREP, LANES), 0) * 2 + rank
    for n in range(ROWS):
        hit = (lane32 < ROWS) & (named == me * SLOTS + ROWS + n)
        code_s[n] = jnp.max(jnp.where(hit, code, -1))
        line_s[n] = jnp.max(jnp.where(hit, lane32, 0))

    slot = known * SLOTS + pltpu.roll(known, LANES - 2 * ROWS, 1)
    goal = jnp.sum(jnp.where(pltpu.roll(own, ROWS, 1) > 0, slot, 0).astype(F32), axis=-1, keepdims=True)
    held = jnp.sum(own.astype(F32), axis=-1, keepdims=True)
    goal = jnp.where(held > 0.0, goal, -1.0)
    goal = jnp.broadcast_to(jnp.concatenate([goal, goal], axis=0), (2 * NREP, LANES)).T[0:1, :]
    line = lax.broadcasted_iota(I32, (NREP * 32, 2 * NREP), 0)
    column = lax.broadcasted_iota(I32, (NREP * 32, 2 * NREP), 1)
    to = ((mx + line // 256) % NX) * NZ + (mz + (line // 32) % NZ) % NZ
    part = line % 32
    for_slot = (part < 16) & (goal == (to * SLOTS + ROWS + part // 2).astype(F32))
    for_own = (part >= 16) & (part < 18) & (column % NREP == to)
    wanted = (for_slot | for_own) & (column // NREP == part % 2)
    route[...] = jnp.where(wanted, 1.0, 0.0).astype(BF16)

    pltpu.make_async_copy(trec, trec, recv_sem.at[2]).wait()
    low = trec[0]
    for n in range(1, TP):
        low = low + trec[n]
    low = low.astype(BF16).astype(F32)
    other = pltpu.roll(low, RANK, 1)
    spread = jnp.concatenate(
        [jnp.where(lane32 < RANK, low, other), jnp.where(lane32 < RANK, other, low)], axis=0
    )
    wide = jnp.where(chosen, jnp.concatenate([spread] * 8, axis=1), 0.0).astype(BF16)
    term = jnp.dot(wide, upv[...], preferred_element_type=F32)
    term = term.astype(BF16)
    head = pl.ds(0, 18)
    for dx in (2, 1, 3, 0):
        lines = pl.ds(dx * NZ * 32, NZ * 32)
        routed = jnp.dot(route[lines], term, preferred_element_type=F32)
        sb3[dx * NZ : (dx + 1) * NZ] = routed.astype(BF16).reshape(NZ, 32, LANES)
        for dz in (4, 3, 5, 2, 6, 1, 7, 0):
            part_of = sb3.at[dx * NZ + dz, head]
            if dx or dz:
                pltpu.make_async_remote_copy(
                    part_of, mvrec.at[me, head], send_sem.at[3], recv_sem.at[3], device_id=(to_x[dx] + to_z[dz], tp),
                    device_id_type=MESH,
                ).start()
            else:
                pltpu.make_async_copy(part_of, mvrec.at[me, head], recv_sem.at[3]).start()

    received(grec, 34, 1)
    for n in range(ROWS):
        safe = jnp.clip(code_s[n], 0, 2 * NREP - 1)
        shift = (LANES - jnp.clip(line_s[n], 0, ROWS - 1) * 16) % LANES
        wq[2 * n : 2 * n + 2, :] = pltpu.roll(grec[safe // 2, 32:48].astype(F32), shift, 1)[0:2]
    column = wq[...].T[0:16, :] * 0.5
    for n in range(ROWS):
        safe = jnp.clip(code_s[n], 0, 2 * NREP - 1)
        one, two = grec[safe // 2, 0:16].astype(F32), grec[safe // 2, 16:32].astype(F32)
        base[n] = jnp.where(code_s[n] >= 0, jnp.where(safe % 2 == 1, two, one), 0.0)
        gain0[n] = jnp.broadcast_to(column[:, 2 * n : 2 * n + 1], (16, LANES))
        gain1[n] = jnp.broadcast_to(column[:, 2 * n + 1 : 2 * n + 2], (16, LANES))
    received(mvrec, 18, 3)
    for r in range(ROWS):
        back = mvrec[owners[r], 16:32].astype(F32)
        value0 = (pvs[r : r + 1, :] + 0.5 * back[0:1]).astype(BF16).astype(F32)
        value1 = (pvs[ROWS + r : ROWS + r + 1, :] + 0.5 * back[1:2]).astype(BF16).astype(F32)
        done = (mixed[r] + wn0s[r] * value0 + wn1s[r] * value1).astype(BF16)
        kept = slots[r] == me * SLOTS + r
        out[r] = jnp.where(kept, done, jnp.zeros((16, LANES), BF16))
    extra = mvrec[0, 0:16].astype(F32)
    for n in range(1, NREP):
        extra = extra + mvrec[n, 0:16].astype(F32)
    for n in range(ROWS):
        added = gain0[n] * extra[2 * n : 2 * n + 1] + gain1[n] * extra[2 * n + 1 : 2 * n + 2]
        out[ROWS + n] = (base[n] + added).astype(BF16)

    def sent(ref, n):
        pltpu.make_async_copy(ref, ref, send_sem.at[n]).wait()

    others = pl.ds(0, NREP - 1)
    sent(sb.at[others, pl.ds(0, 18)], 0)
    sent(mrec.at[others], 4)
    sent(sb4.at[others, pl.ds(0, 34)], 1)
    sent(trec.at[pl.ds(0, TP - 1)], 2)
    sent(sb3.at[others, pl.ds(0, 18)], 3)


def shards(hidden, queries, wk, wv, down, up, ridx, home, table, lengths, serve, kc, vc):
    hid = hidden.reshape(ROWS, 2, CHUNKS, LANES).transpose(0, 2, 1, 3).reshape(ROWS, LANES, LANES)
    qin = queries.reshape(ROWS, 2, 8, LANES).transpose(0, 2, 1, 3).reshape(ROWS, 16, LANES)
    dn = jnp.swapaxes(down, 1, 2)
    upr = up.reshape(ADP * RANK, LANES)
    vmem, smem = pltpu.VMEM, pltpu.SMEM
    scratch = [
        vmem((ROWS, LANES, LANES), BF16), vmem((ROWS, 16, LANES), BF16), vmem((8192, LANES), BF16), vmem((8192, LANES), BF16),
        vmem((ADP, RANK, 1024), BF16), vmem((ADP * RANK, LANES), BF16), vmem((64, LANES, LANES), BF16), vmem((64, LANES, LANES), BF16),
        smem((8,), I32), smem((512,), I32), smem((8, 8), I32), smem((1, 8), I32), smem((8,), I32),
        vmem((ROWS * LANES, LANES), F32), vmem((16, 8192), BF16),
        vmem((NREP, 32, LANES), BF16), vmem((NREP, 32, LANES), BF16),
        vmem((NREP * 16, LANES), F32), vmem((NREP * 16, LANES), F32), vmem((2 * NREP, 1024), BF16),
        vmem((1, LANES), I32), vmem((NREP, 1, LANES), I32),
        vmem((NREP, LANES), F32), vmem((TP, NREP, LANES), F32),
        vmem((ROWS, 16, LANES), F32), vmem((ROWS, 16, LANES), F32), vmem((ROWS, 16, LANES), F32),
        vmem((16, LANES), F32), vmem((16, LANES), F32),
        vmem((ROWS, 16, LANES), BF16), vmem((ROWS, 16, LANES), F32),
        vmem((NREP, 48, LANES), BF16), vmem((NREP, 48, LANES), BF16),
        vmem((NREP * 32, 2 * NREP), BF16), vmem((NREP, 32, LANES), BF16), vmem((NREP, 32, LANES), BF16),
        vmem((ROWS, 16, LANES), F32), vmem((ROWS, 16, LANES), F32), vmem((ROWS, 16, LANES), F32),
        vmem((8, LANES), I32), smem((8, LANES), I32), smem((ROWS,), I32), smem((ROWS,), I32), vmem((16, LANES), F32),
        pltpu.SemaphoreType.DMA((14,)), pltpu.SemaphoreType.DMA((5,)), pltpu.SemaphoreType.DMA((5,)),
    ]
    hid, qin, wk, wv, dn, upr, ridx, home, table, lengths, serve, kc, vc = (pltpu.with_memory_space_constraint(a, pltpu.HBM) for a in (hid, qin, wk, wv, dn, upr, ridx, home, table, lengths, serve, kc, vc))
    result = pl.pallas_call(
        kernel,
        out_shape=jax.ShapeDtypeStruct((SLOTS, 16, LANES), BF16),
        in_specs=[pl.BlockSpec(memory_space=pltpu.HBM)] * 13,
        out_specs=pl.BlockSpec(memory_space=pltpu.VMEM),
        scratch_shapes=scratch,
        compiler_params=pltpu.CompilerParams(
            collective_id=0, has_side_effects=True, vmem_limit_bytes=48 << 20
        ),
        name="decode",
    )(hid, qin, wk, wv, dn, upr, ridx, home, table, lengths, serve, kc, vc)
    return result.reshape(SLOTS, 8, 2, LANES).transpose(0, 2, 1, 3).reshape(SLOTS, 2, 1024)


def solution(mesh):
    placed = (
        P("rep", None, None),
        P("rep", None, "tp"),
        P(None, "tp"),
        P(None, "tp"),
        P("rep", "tp", None),
        P("rep", None, "tp"),
        P("rep"),
        P(),
        P("rep", None),
        P("rep", None),
        P("rep"),
        P("rep", None, "tp"),
        P("rep", None, "tp"),
    )
    return jax.shard_map(
        shards, mesh=mesh, in_specs=placed, out_specs=P("rep", None, "tp"), check_vma=False
    )
```

```python
import functools
import math

import jax
import jax.numpy as jnp
from jax import lax
from jax.experimental import pallas as pl
from jax.experimental.pallas import tpu as pltpu
from jax.sharding import PartitionSpec as P

MESH = pl.DeviceIdType.MESH
F32, BF16, I32 = jnp.float32, jnp.bfloat16, jnp.int32

NX, NZ, TP = 4, 8, 8
NREP = NX * NZ
ROWS, SLOTS, ADP, RANK = 8, 16, 16, 64
LANES = 128
CHUNKS = 64
NT = (((1,), (1,)), ((), ()))
LOG_BASE = math.log(1000000.0)
FAR_FIRST = sorted(
    [(x, z) for x in range(NX) for z in range(NZ) if x or z],
    key=lambda o: (-min(o[1], NZ - o[1]), -min(o[0], NX - o[0])),
)


def kernel(
    hid, qin, wk, wv, dn, up, ridx, home, table, length, serve, kc, vc,
    out,
    hidv, qv, wkv, wvv, dnv, upv, kv, vv, ridx_s, home_s, table_s, length_s, serve_s,
    hf, xl, sb, arr, af, ai, xs, mb, mrec, tb, trec, mixed, wn0s, wn1s, nkf, pvs, plain, gains, sb4, grec,
    route, sb3, mvrec, base, gain0, gain1, tab, tab_s, code_s, line_s, wq, in_sem, send_sem, recv_sem,
):
    me = lax.axis_index("rep")
    tp = lax.axis_index("tp")
    mx, mz = me // NZ, me % NZ

    to_x = [((mx + n) % NX) * NZ for n in range(NX)]
    to_z = [(mz + n) % NZ for n in range(NZ)]

    def peers(do):
        for dx, dz in FAR_FIRST:
            do(to_x[dx] + to_z[dz])

    def tp_peers(do):
        for a in (4, 5, 3, 2, 6, 1, 7):
            do((tp + a) % TP)

    bar = pltpu.get_barrier_semaphore()
    peers(lambda d: pl.semaphore_signal(bar, inc=1, device_id=(d, tp), device_id_type=MESH))
    tp_peers(lambda d: pl.semaphore_signal(bar, inc=1, device_id=(me, d), device_id_type=MESH))

    pairs = [
        (ridx, ridx_s), (home, home_s), (serve, serve_s), (hid, hidv), (length, length_s), (table, table_s),
        (wk, wkv), (wv, wvv), (qin, qv), (kc, kv), (vc, vv), (dn, dnv), (up, upv),
    ]
    loads = [pltpu.make_async_copy(s, d, in_sem.at[n]) for n, (s, d) in enumerate(pairs)]
    for c in loads:
        c.start()
    (l_ridx, l_home, l_serve, l_hid, l_len, l_tab, l_wk, l_wv, l_q, l_k, l_v, l_dn, l_up) = loads

    l_hid.wait()
    hf[...] = hidv[...].reshape(ROWS * LANES, LANES).astype(F32)
    for c in range(CHUNKS):
        both = [hf[pl.ds(2 * c + t, ROWS, stride=LANES), :] for t in range(2)]
        xl[:, c * LANES : (c + 1) * LANES] = jnp.concatenate(both, axis=0).astype(BF16)
    l_ridx.wait()
    l_home.wait()
    l_serve.wait()
    homes = [home_s[ridx_s[i]] for i in range(ROWS)]
    owners = [h // ADP for h in homes]
    slots = [serve_s[i] for i in range(ROWS)]
    lane1 = lax.broadcasted_iota(I32, (1, LANES), 1)
    meta = jnp.zeros((1, LANES), I32)
    for i in range(ROWS):
        for n, value in enumerate((owners[i], slots[i] // SLOTS, homes[i] % ADP, slots[i] % SLOTS)):
            meta = jnp.where(lane1 == n * ROWS + i, value, meta)
    line = jnp.full((1, LANES), -1, I32)
    for i in range(ROWS):
        line = jnp.where(lane1 == i, slots[i], line)
    mb[...] = line
    meta = jnp.broadcast_to(meta.astype(F32), (16, LANES)).astype(BF16)
    mine = pl.multiple_of(tp * 16, 16)

    targets = [s // SLOTS for s in slots]
    none = jnp.zeros((1, LANES), I32)
    to_home, first, second, count = none, none, none, none
    for i in range(ROWS):
        to_home = jnp.where(lane1 == owners[i], i, to_home)
        here = lane1 == targets[i]
        first = jnp.where(here & (count == 0), i, first)
        second = jnp.where(here & (count == 1), i, second)
        count = count + here.astype(I32)
    tab[...] = jnp.zeros((8, LANES), I32)
    tab[0:1, :] = to_home
    tab[1:2, :] = first
    tab[2:3, :] = second
    to_smem = pltpu.make_async_copy(tab, tab_s, in_sem.at[13])
    to_smem.start()
    l_wk.wait()
    new_keys = jnp.dot(xl[...], wkv[...], preferred_element_type=F32)
    l_len.wait()
    row16 = lax.broadcasted_iota(I32, (2 * ROWS, LANES), 0)
    lane16 = lax.broadcasted_iota(I32, (2 * ROWS, LANES), 1)
    position = jnp.zeros((2 * ROWS, LANES), I32)
    for i in range(ROWS):
        for t in range(2):
            position = jnp.where(row16 == t * ROWS + i, length_s[0, i] + t, position)
    half = (lane16 % (LANES // 2)).astype(F32)
    angle = position.astype(F32) * jnp.exp(half * (-2.0 * LOG_BASE / LANES))
    turned = pltpu.roll(new_keys, LANES // 2, 1)
    sine = jnp.where(lane16 < LANES // 2, -jnp.sin(angle), jnp.sin(angle))
    nkf[...] = (new_keys * jnp.cos(angle) + turned * sine).astype(BF16).astype(F32)
    l_wv.wait()
    pvs[...] = jnp.dot(xl[...], wvv[...], preferred_element_type=F32)

    to_smem.wait()

    def fill(d, carry):
        sb[d, 0:16] = hidv[tab_s[0, d], pl.ds(mine, 16), :]
        sb[d, 16:32] = meta
        return carry

    lax.fori_loop(0, NREP, fill, 0)

    pl.semaphore_wait(bar, NREP - 1 + TP - 1)

    def exchange(src, dst, lines, n):
        part = pl.ds(0, lines)

        def one(d):
            pltpu.make_async_remote_copy(
                src.at[d, part], dst.at[me, part], send_sem.at[n], recv_sem.at[n], device_id=(d, tp), device_id_type=MESH
            ).start()

        peers(one)
        pltpu.make_async_copy(src.at[me, part], dst.at[me, part], recv_sem.at[n]).start()

    def received(dst, lines, n):
        every = dst.at[:, pl.ds(0, lines)]
        pltpu.make_async_copy(every, every, recv_sem.at[n]).wait()

    exchange(sb, arr, 18, 0)

    def tell(d):
        pltpu.make_async_remote_copy(
            mb, mrec.at[me], send_sem.at[4], recv_sem.at[4], device_id=(d, tp), device_id_type=MESH
        ).start()

    peers(tell)
    pltpu.make_async_copy(mb, mrec.at[me], recv_sem.at[4]).start()

    l_tab.wait()
    l_q.wait()
    l_k.wait()
    l_v.wait()
    scale = LANES ** (-0.5)
    span = ROWS * LANES
    token = lax.broadcasted_iota(I32, (16, 1), 0) % 2
    place = lax.broadcasted_iota(I32, (16, span), 1)

    def attend(r, carry):
        q = qv[r]
        pages = [table_s[r, n] for n in range(8)]
        keys = jnp.concatenate([kv[p] for p in pages], axis=0)
        old = lax.dot_general(q, keys, NT, preferred_element_type=F32) * scale
        old = jnp.where(place < length_s[0, r], old, -jnp.inf)
        qf = q.astype(F32)
        new0 = jnp.sum(qf * nkf[pl.ds(r, 1), :], axis=-1, keepdims=True) * scale
        new1 = jnp.sum(qf * nkf[pl.ds(ROWS + r, 1), :], axis=-1, keepdims=True) * scale
        new1 = jnp.where(token == 1, new1, -jnp.inf)
        peak = jnp.maximum(jnp.max(old, axis=-1, keepdims=True), jnp.maximum(new0, new1))
        eo, e0, e1 = jnp.exp(old - peak), jnp.exp(new0 - peak), jnp.exp(new1 - peak)
        total = jnp.sum(eo, axis=-1, keepdims=True) + e0 + e1
        weights = (eo / total).astype(BF16)
        values = jnp.concatenate([vv[p] for p in pages], axis=0)
        mixed[r] = jnp.dot(weights, values, preferred_element_type=F32)
        w0 = jnp.broadcast_to((e0 / total).astype(BF16).astype(F32), (16, LANES))
        w1 = jnp.broadcast_to((e1 / total).astype(BF16).astype(F32), (16, LANES))
        wn0s[r] = w0
        wn1s[r] = w1
        fresh = w0 * pvs[pl.ds(r, 1), :] + w1 * pvs[pl.ds(ROWS + r, 1), :]
        plain[r] = (mixed[r] + fresh).astype(BF16)
        gains[r] = jnp.where(lane16 == 0, w0, w1)
        return carry

    def several(n, carry):
        for u in range(4):
            attend(n * 4 + u, carry)
        return carry

    lax.fori_loop(0, ROWS // 4, several, 0)

    gain_lines = gains[...].reshape(ROWS * 16, LANES).T[0:16, :].astype(BF16)

    def moved(d, carry):
        one, two = tab_s[1, d], tab_s[2, d]
        sb4[d, 0:16] = plain[one]
        sb4[d, 16:32] = plain[two]
        sb4[d, 32:48] = gain_lines
        return carry

    lax.fori_loop(0, NREP, moved, 0)
    exchange(sb4, grec, 34, 1)

    l_dn.wait()
    l_up.wait()
    received(arr, 18, 0)
    af[...] = arr[:, 0:16, :].reshape(NREP * 16, LANES).astype(F32)
    ai[...] = arr[:, 16:32, :].reshape(NREP * 16, LANES).astype(F32)
    for c in range(8):
        for t in range(2):
            piece = af[pl.ds(2 * c + t, NREP, stride=16), :]
            xs[t * NREP : (t + 1) * NREP, c * LANES : (c + 1) * LANES] = piece.astype(BF16)
    every = lax.dot_general(xs[...], dnv[...].reshape(ADP * RANK, 8 * LANES), NT, preferred_element_type=F32)
    known = ai[pl.ds(0, NREP, stride=16), :].astype(I32)
    lane32 = lax.broadcasted_iota(I32, (NREP, LANES), 1)
    own = ((known == me) & (lane32 < ROWS)).astype(I32)
    within = jnp.where(pltpu.roll(own, 2 * ROWS, 1) > 0, known, 0)
    within = jnp.sum(within.astype(F32), axis=-1, keepdims=True).astype(I32)
    pick = jnp.concatenate([within, within], axis=0)
    block = lax.broadcasted_iota(I32, (2 * NREP, ADP * RANK), 1) // RANK
    chosen = block == pick
    every = jnp.where(chosen, every, 0.0)
    folded = every[:, :LANES]
    for v in range(1, 8):
        folded = folded + every[:, v * LANES : (v + 1) * LANES]
    folded = folded + pltpu.roll(folded, RANK, 1)
    tb[...] = jnp.where(lane32 < RANK, folded[:NREP], folded[NREP:])

    def to_tp(d):
        pltpu.make_async_remote_copy(
            tb, trec.at[tp], send_sem.at[2], recv_sem.at[2], device_id=(me, d), device_id_type=MESH
        ).start()

    tp_peers(to_tp)
    pltpu.make_async_copy(tb, trec.at[tp], recv_sem.at[2]).start()

    pltpu.make_async_copy(mrec, mrec, recv_sem.at[4]).wait()
    named = mrec[:, 0, :]
    target = named // SLOTS
    rank = jnp.zeros((NREP, LANES), I32)
    for back in range(1, ROWS):
        same = (pltpu.roll(target, back, 1) == target) & (lane32 >= back)
        rank = rank + same.astype(I32)
    code = lax.broadcasted_iota(I32, (NREP, LANES), 0) * 2 + rank
    for n in range(ROWS):
        hit = (lane32 < ROWS) & (named == me * SLOTS + ROWS + n)
        code_s[n] = jnp.max(jnp.where(hit, code, -1))
        line_s[n] = jnp.max(jnp.where(hit, lane32, 0))

    slot = known * SLOTS + pltpu.roll(known, LANES - 2 * ROWS, 1)
    goal = jnp.sum(jnp.where(pltpu.roll(own, ROWS, 1) > 0, slot, 0).astype(F32), axis=-1, keepdims=True)
    held = jnp.sum(own.astype(F32), axis=-1, keepdims=True)
    goal = jnp.where(held > 0.0, goal, -1.0)
    goal = jnp.broadcast_to(jnp.concatenate([goal, goal], axis=0), (2 * NREP, LANES)).T[0:1, :]
    line = lax.broadcasted_iota(I32, (NREP * 32, 2 * NREP), 0)
    column = lax.broadcasted_iota(I32, (NREP * 32, 2 * NREP), 1)
    to = ((mx + line // 256) % NX) * NZ + (mz + (line // 32) % NZ) % NZ
    part = line % 32
    for_slot = (part < 16) & (goal == (to * SLOTS + ROWS + part // 2).astype(F32))
    for_own = (part >= 16) & (part < 18) & (column % NREP == to)
    wanted = (for_slot | for_own) & (column // NREP == part % 2)
    route[...] = jnp.where(wanted, 1.0, 0.0).astype(BF16)

    pltpu.make_async_copy(trec, trec, recv_sem.at[2]).wait()
    low = trec[0]
    for n in range(1, TP):
        low = low + trec[n]
    low = low.astype(BF16).astype(F32)
    other = pltpu.roll(low, RANK, 1)
    spread = jnp.concatenate(
        [jnp.where(lane32 < RANK, low, other), jnp.where(lane32 < RANK, other, low)], axis=0
    )
    wide = jnp.where(chosen, jnp.concatenate([spread] * 8, axis=1), 0.0).astype(BF16)
    term = jnp.dot(wide, upv[...], preferred_element_type=F32)
    term = term.astype(BF16)
    head = pl.ds(0, 18)
    for dx in (2, 1, 3, 0):
        lines = pl.ds(dx * NZ * 32, NZ * 32)
        routed = jnp.dot(route[lines], term, preferred_element_type=F32)
        sb3[dx * NZ : (dx + 1) * NZ] = routed.astype(BF16).reshape(NZ, 32, LANES)
        for dz in (4, 3, 5, 2, 6, 1, 7, 0):
            part_of = sb3.at[dx * NZ + dz, head]
            if dx or dz:
                pltpu.make_async_remote_copy(
                    part_of, mvrec.at[me, head], send_sem.at[3], recv_sem.at[3], device_id=(to_x[dx] + to_z[dz], tp),
                    device_id_type=MESH,
                ).start()
            else:
                pltpu.make_async_copy(part_of, mvrec.at[me, head], recv_sem.at[3]).start()

    received(grec, 34, 1)
    for n in range(ROWS):
        safe = jnp.clip(code_s[n], 0, 2 * NREP - 1)
        shift = (LANES - jnp.clip(line_s[n], 0, ROWS - 1) * 16) % LANES
        wq[2 * n : 2 * n + 2, :] = pltpu.roll(grec[safe // 2, 32:48].astype(F32), shift, 1)[0:2]
    column = wq[...].T[0:16, :] * 0.5
    for n in range(ROWS):
        safe = jnp.clip(code_s[n], 0, 2 * NREP - 1)
        one, two = grec[safe // 2, 0:16].astype(F32), grec[safe // 2, 16:32].astype(F32)
        base[n] = jnp.where(code_s[n] >= 0, jnp.where(safe % 2 == 1, two, one), 0.0)
        gain0[n] = jnp.broadcast_to(column[:, 2 * n : 2 * n + 1], (16, LANES))
        gain1[n] = jnp.broadcast_to(column[:, 2 * n + 1 : 2 * n + 2], (16, LANES))
    received(mvrec, 18, 3)
    for r in range(ROWS):
        back = mvrec[owners[r], 16:32].astype(F32)
        value0 = (pvs[r : r + 1, :] + 0.5 * back[0:1]).astype(BF16).astype(F32)
        value1 = (pvs[ROWS + r : ROWS + r + 1, :] + 0.5 * back[1:2]).astype(BF16).astype(F32)
        done = (mixed[r] + wn0s[r] * value0 + wn1s[r] * value1).astype(BF16)
        kept = slots[r] == me * SLOTS + r
        out[r] = jnp.where(kept, done, jnp.zeros((16, LANES), BF16))
    extra = mvrec[0, 0:16].astype(F32)
    for n in range(1, NREP):
        extra = extra + mvrec[n, 0:16].astype(F32)
    for n in range(ROWS):
        added = gain0[n] * extra[2 * n : 2 * n + 1] + gain1[n] * extra[2 * n + 1 : 2 * n + 2]
        out[ROWS + n] = (base[n] + added).astype(BF16)

    def sent(ref, n):
        pltpu.make_async_copy(ref, ref, send_sem.at[n]).wait()

    others = pl.ds(0, NREP - 1)
    sent(sb.at[others, pl.ds(0, 18)], 0)
    sent(mrec.at[others], 4)
    sent(sb4.at[others, pl.ds(0, 34)], 1)
    sent(trec.at[pl.ds(0, TP - 1)], 2)
    sent(sb3.at[others, pl.ds(0, 18)], 3)


def shards(hidden, queries, wk, wv, down, up, ridx, home, table, lengths, serve, kc, vc):
    hid = hidden.reshape(ROWS, 2, CHUNKS, LANES).transpose(0, 2, 1, 3).reshape(ROWS, LANES, LANES)
    qin = queries.reshape(ROWS, 2, 8, LANES).transpose(0, 2, 1, 3).reshape(ROWS, 16, LANES)
    dn = jnp.swapaxes(down, 1, 2)
    upr = up.reshape(ADP * RANK, LANES)
    vmem, smem = pltpu.VMEM, pltpu.SMEM
    scratch = [
        vmem((ROWS, LANES, LANES), BF16), vmem((ROWS, 16, LANES), BF16), vmem((8192, LANES), BF16), vmem((8192, LANES), BF16),
        vmem((ADP, RANK, 1024), BF16), vmem((ADP * RANK, LANES), BF16), vmem((64, LANES, LANES), BF16), vmem((64, LANES, LANES), BF16),
        smem((8,), I32), smem((512,), I32), smem((8, 8), I32), smem((1, 8), I32), smem((8,), I32),
        vmem((ROWS * LANES, LANES), F32), vmem((16, 8192), BF16),
        vmem((NREP, 32, LANES), BF16), vmem((NREP, 32, LANES), BF16),
        vmem((NREP * 16, LANES), F32), vmem((NREP * 16, LANES), F32), vmem((2 * NREP, 1024), BF16),
        vmem((1, LANES), I32), vmem((NREP, 1, LANES), I32),
        vmem((NREP, LANES), F32), vmem((TP, NREP, LANES), F32),
        vmem((ROWS, 16, LANES), F32), vmem((ROWS, 16, LANES), F32), vmem((ROWS, 16, LANES), F32),
        vmem((16, LANES), F32), vmem((16, LANES), F32),
        vmem((ROWS, 16, LANES), BF16), vmem((ROWS, 16, LANES), F32),
        vmem((NREP, 48, LANES), BF16), vmem((NREP, 48, LANES), BF16),
        vmem((NREP * 32, 2 * NREP), BF16), vmem((NREP, 32, LANES), BF16), vmem((NREP, 32, LANES), BF16),
        vmem((ROWS, 16, LANES), F32), vmem((ROWS, 16, LANES), F32), vmem((ROWS, 16, LANES), F32),
        vmem((8, LANES), I32), smem((8, LANES), I32), smem((ROWS,), I32), smem((ROWS,), I32), vmem((16, LANES), F32),
        pltpu.SemaphoreType.DMA((14,)), pltpu.SemaphoreType.DMA((5,)), pltpu.SemaphoreType.DMA((5,)),
    ]
    hid, qin, wk, wv, dn, upr, ridx, home, table, lengths, serve, kc, vc = (pltpu.with_memory_space_constraint(a, pltpu.HBM) for a in (hid, qin, wk, wv, dn, upr, ridx, home, table, lengths, serve, kc, vc))
    result = pl.pallas_call(
        kernel,
        out_shape=jax.ShapeDtypeStruct((SLOTS, 16, LANES), BF16),
        in_specs=[pl.BlockSpec(memory_space=pltpu.HBM)] * 13,
        out_specs=pl.BlockSpec(memory_space=pltpu.VMEM),
        scratch_shapes=scratch,
        compiler_params=pltpu.CompilerParams(
            collective_id=0, has_side_effects=True, vmem_limit_bytes=48 << 20
        ),
        name="decode",
    )(hid, qin, wk, wv, dn, upr, ridx, home, table, lengths, serve, kc, vc)
    return result.reshape(SLOTS, 8, 2, LANES).transpose(0, 2, 1, 3).reshape(SLOTS, 2, 1024)


def solution(mesh):
    placed = (
        P("rep", None, None),
        P("rep", None, "tp"),
        P(None, "tp"),
        P(None, "tp"),
        P("rep", "tp", None),
        P("rep", None, "tp"),
        P("rep"),
        P(),
        P("rep", None),
        P("rep", None),
        P("rep"),
        P("rep", None, "tp"),
        P("rep", None, "tp"),
    )
    return jax.shard_map(
        shards, mesh=mesh, in_specs=placed, out_specs=P("rep", None, "tp"), check_vma=False
    )
```

```python
import functools
import math

import jax
import jax.numpy as jnp
from jax import lax
from jax.experimental import pallas as pl
from jax.experimental.pallas import tpu as pltpu
from jax.sharding import PartitionSpec as P

MESH = pl.DeviceIdType.MESH
F32, BF16, I32 = jnp.float32, jnp.bfloat16, jnp.int32

NX, NZ, TP = 4, 8, 8
NREP = NX * NZ
ROWS, SLOTS, ADP, RANK = 8, 16, 16, 64
LANES = 128
CHUNKS = 64
NT = (((1,), (1,)), ((), ()))
LOG_BASE = math.log(1000000.0)
FAR_FIRST = sorted(
    [(x, z) for x in range(NX) for z in range(NZ) if x or z],
    key=lambda o: (-min(o[1], NZ - o[1]), -min(o[0], NX - o[0])),
)


def kernel(
    hid, qin, wk, wv, dn, up, ridx, home, table, length, serve, kc, vc,
    out,
    hidv, qv, wkv, wvv, dnv, upv, kv, vv, ridx_s, home_s, table_s, length_s, serve_s,
    hf, xl, sb, arr, af, ai, xs, mb, mrec, tb, trec, mixed, wn0s, wn1s, nkf, pvs, plain, gains, sb4, grec,
    route, sb3, mvrec, base, gain0, gain1, tab, tab_s, code_s, line_s, wq, in_sem, send_sem, recv_sem,
):
    me = lax.axis_index("rep")
    tp = lax.axis_index("tp")
    mx, mz = me // NZ, me % NZ

    to_x = [((mx + n) % NX) * NZ for n in range(NX)]
    to_z = [(mz + n) % NZ for n in range(NZ)]

    def peers(do):
        for dx, dz in FAR_FIRST:
            do(to_x[dx] + to_z[dz])

    def tp_peers(do):
        for a in (4, 5, 3, 2, 6, 1, 7):
            do((tp + a) % TP)

    bar = pltpu.get_barrier_semaphore()
    peers(lambda d: pl.semaphore_signal(bar, inc=1, device_id=(d, tp), device_id_type=MESH))
    tp_peers(lambda d: pl.semaphore_signal(bar, inc=1, device_id=(me, d), device_id_type=MESH))

    pairs = [
        (ridx, ridx_s), (home, home_s), (serve, serve_s), (hid, hidv), (length, length_s), (table, table_s),
        (wk, wkv), (wv, wvv), (qin, qv), (kc, kv), (vc, vv), (dn, dnv), (up, upv),
    ]
    loads = [pltpu.make_async_copy(s, d, in_sem.at[n]) for n, (s, d) in enumerate(pairs)]
    for c in loads:
        c.start()
    (l_ridx, l_home, l_serve, l_hid, l_len, l_tab, l_wk, l_wv, l_q, l_k, l_v, l_dn, l_up) = loads

    l_hid.wait()
    hf[...] = hidv[...].reshape(ROWS * LANES, LANES).astype(F32)
    for c in range(CHUNKS):
        both = [hf[pl.ds(2 * c + t, ROWS, stride=LANES), :] for t in range(2)]
        xl[:, c * LANES : (c + 1) * LANES] = jnp.concatenate(both, axis=0).astype(BF16)
    l_ridx.wait()
    l_home.wait()
    l_serve.wait()
    homes = [home_s[ridx_s[i]] for i in range(ROWS)]
    owners = [h // ADP for h in homes]
    slots = [serve_s[i] for i in range(ROWS)]
    lane1 = lax.broadcasted_iota(I32, (1, LANES), 1)
    meta = jnp.zeros((1, LANES), I32)
    for i in range(ROWS):
        for n, value in enumerate((owners[i], slots[i] // SLOTS, homes[i] % ADP, slots[i] % SLOTS)):
            meta = jnp.where(lane1 == n * ROWS + i, value, meta)
    line = jnp.full((1, LANES), -1, I32)
    for i in range(ROWS):
        line = jnp.where(lane1 == i, slots[i], line)
    mb[...] = line
    meta = jnp.broadcast_to(meta.astype(F32), (16, LANES)).astype(BF16)
    mine = pl.multiple_of(tp * 16, 16)

    targets = [s // SLOTS for s in slots]
    none = jnp.zeros((1, LANES), I32)
    to_home, first, second, count = none, none, none, none
    for i in range(ROWS):
        to_home = jnp.where(lane1 == owners[i], i, to_home)
        here = lane1 == targets[i]
        first = jnp.where(here & (count == 0), i, first)
        second = jnp.where(here & (count == 1), i, second)
        count = count + here.astype(I32)
    tab[...] = jnp.zeros((8, LANES), I32)
    tab[0:1, :] = to_home
    tab[1:2, :] = first
    tab[2:3, :] = second
    to_smem = pltpu.make_async_copy(tab, tab_s, in_sem.at[13])
    to_smem.start()
    l_wk.wait()
    new_keys = jnp.dot(xl[...], wkv[...], preferred_element_type=F32)
    l_len.wait()
    row16 = lax.broadcasted_iota(I32, (2 * ROWS, LANES), 0)
    lane16 = lax.broadcasted_iota(I32, (2 * ROWS, LANES), 1)
    position = jnp.zeros((2 * ROWS, LANES), I32)
    for i in range(ROWS):
        for t in range(2):
            position = jnp.where(row16 == t * ROWS + i, length_s[0, i] + t, position)
    half = (lane16 % (LANES // 2)).astype(F32)
    angle = position.astype(F32) * jnp.exp(half * (-2.0 * LOG_BASE / LANES))
    turned = pltpu.roll(new_keys, LANES // 2, 1)
    sine = jnp.where(lane16 < LANES // 2, -jnp.sin(angle), jnp.sin(angle))
    nkf[...] = (new_keys * jnp.cos(angle) + turned * sine).astype(BF16).astype(F32)
    l_wv.wait()
    pvs[...] = jnp.dot(xl[...], wvv[...], preferred_element_type=F32)

    to_smem.wait()

    def fill(d, carry):
        sb[d, 0:16] = hidv[tab_s[0, d], pl.ds(mine, 16), :]
        sb[d, 16:32] = meta
        return carry

    lax.fori_loop(0, NREP, fill, 0)

    pl.semaphore_wait(bar, NREP - 1 + TP - 1)

    def exchange(src, dst, lines, n):
        part = pl.ds(0, lines)

        def one(d):
            pltpu.make_async_remote_copy(
                src.at[d, part], dst.at[me, part], send_sem.at[n], recv_sem.at[n], device_id=(d, tp), device_id_type=MESH
            ).start()

        peers(one)
        pltpu.make_async_copy(src.at[me, part], dst.at[me, part], recv_sem.at[n]).start()

    def received(dst, lines, n):
        every = dst.at[:, pl.ds(0, lines)]
        pltpu.make_async_copy(every, every, recv_sem.at[n]).wait()

    exchange(sb, arr, 18, 0)

    def tell(d):
        pltpu.make_async_remote_copy(
            mb, mrec.at[me], send_sem.at[4], recv_sem.at[4], device_id=(d, tp), device_id_type=MESH
        ).start()

    peers(tell)
    pltpu.make_async_copy(mb, mrec.at[me], recv_sem.at[4]).start()

    l_tab.wait()
    l_q.wait()
    l_k.wait()
    l_v.wait()
    scale = LANES ** (-0.5)
    span = ROWS * LANES
    token = lax.broadcasted_iota(I32, (16, 1), 0) % 2
    place = lax.broadcasted_iota(I32, (16, span), 1)

    def attend(r, carry):
        q = qv[r]
        pages = [table_s[r, n] for n in range(8)]
        keys = jnp.concatenate([kv[p] for p in pages], axis=0)
        old = lax.dot_general(q, keys, NT, preferred_element_type=F32) * scale
        old = jnp.where(place < length_s[0, r], old, -jnp.inf)
        qf = q.astype(F32)
        new0 = jnp.sum(qf * nkf[pl.ds(r, 1), :], axis=-1, keepdims=True) * scale
        new1 = jnp.sum(qf * nkf[pl.ds(ROWS + r, 1), :], axis=-1, keepdims=True) * scale
        new1 = jnp.where(token == 1, new1, -jnp.inf)
        peak = jnp.maximum(jnp.max(old, axis=-1, keepdims=True), jnp.maximum(new0, new1))
        eo, e0, e1 = jnp.exp(old - peak), jnp.exp(new0 - peak), jnp.exp(new1 - peak)
        total = jnp.sum(eo, axis=-1, keepdims=True) + e0 + e1
        weights = (eo / total).astype(BF16)
        values = jnp.concatenate([vv[p] for p in pages], axis=0)
        mixed[r] = jnp.dot(weights, values, preferred_element_type=F32)
        w0 = jnp.broadcast_to((e0 / total).astype(BF16).astype(F32), (16, LANES))
        w1 = jnp.broadcast_to((e1 / total).astype(BF16).astype(F32), (16, LANES))
        wn0s[r] = w0
        wn1s[r] = w1
        fresh = w0 * pvs[pl.ds(r, 1), :] + w1 * pvs[pl.ds(ROWS + r, 1), :]
        plain[r] = (mixed[r] + fresh).astype(BF16)
        gains[r] = jnp.where(lane16 == 0, w0, w1)
        return carry

    def several(n, carry):
        for u in range(4):
            attend(n * 4 + u, carry)
        return carry

    lax.fori_loop(0, ROWS // 4, several, 0)

    gain_lines = gains[...].reshape(ROWS * 16, LANES).T[0:16, :].astype(BF16)

    def moved(d, carry):
        one, two = tab_s[1, d], tab_s[2, d]
        sb4[d, 0:16] = plain[one]
        sb4[d, 16:32] = plain[two]
        sb4[d, 32:48] = gain_lines
        return carry

    lax.fori_loop(0, NREP, moved, 0)
    exchange(sb4, grec, 34, 1)

    l_dn.wait()
    l_up.wait()
    received(arr, 18, 0)
    af[...] = arr[:, 0:16, :].reshape(NREP * 16, LANES).astype(F32)
    ai[...] = arr[:, 16:32, :].reshape(NREP * 16, LANES).astype(F32)
    for c in range(8):
        for t in range(2):
            piece = af[pl.ds(2 * c + t, NREP, stride=16), :]
            xs[t * NREP : (t + 1) * NREP, c * LANES : (c + 1) * LANES] = piece.astype(BF16)
    known = ai[pl.ds(0, NREP, stride=16), :].astype(I32)
    lane32 = lax.broadcasted_iota(I32, (NREP, LANES), 1)
    own = ((known == me) & (lane32 < ROWS)).astype(I32)
    within = jnp.where(pltpu.roll(own, 2 * ROWS, 1) > 0, known, 0)
    within = jnp.sum(within.astype(F32), axis=-1, keepdims=True).astype(I32)
    pick = jnp.concatenate([within, within], axis=0)
    block = lax.broadcasted_iota(I32, (2 * NREP, ADP * RANK), 1) // RANK
    chosen = block == pick
    folded = jnp.zeros((2 * NREP, LANES), F32)
    for g in range(4):
        some = dnv[4 * g : 4 * g + 4].reshape(4 * RANK, 8 * LANES)
        some = lax.dot_general(xs[...], some, NT, preferred_element_type=F32)
        some = jnp.where(chosen[:, g * 4 * RANK : (g + 1) * 4 * RANK], some, 0.0)
        folded = folded + some[:, :LANES] + some[:, LANES:]
    folded = folded + pltpu.roll(folded, RANK, 1)
    tb[...] = jnp.where(lane32 < RANK, folded[:NREP], folded[NREP:])

    def to_tp(d):
        pltpu.make_async_remote_copy(
            tb, trec.at[tp], send_sem.at[2], recv_sem.at[2], device_id=(me, d), device_id_type=MESH
        ).start()

    tp_peers(to_tp)
    pltpu.make_async_copy(tb, trec.at[tp], recv_sem.at[2]).start()

    pltpu.make_async_copy(mrec, mrec, recv_sem.at[4]).wait()
    named = mrec[:, 0, :]
    target = named // SLOTS
    rank = jnp.zeros((NREP, LANES), I32)
    for back in range(1, ROWS):
        same = (pltpu.roll(target, back, 1) == target) & (lane32 >= back)
        rank = rank + same.astype(I32)
    code = lax.broadcasted_iota(I32, (NREP, LANES), 0) * 2 + rank
    for n in range(ROWS):
        hit = (lane32 < ROWS) & (named == me * SLOTS + ROWS + n)
        code_s[n] = jnp.max(jnp.where(hit, code, -1))
        line_s[n] = jnp.max(jnp.where(hit, lane32, 0))

    slot = known * SLOTS + pltpu.roll(known, LANES - 2 * ROWS, 1)
    goal = jnp.sum(jnp.where(pltpu.roll(own, ROWS, 1) > 0, slot, 0).astype(F32), axis=-1, keepdims=True)
    held = jnp.sum(own.astype(F32), axis=-1, keepdims=True)
    goal = jnp.where(held > 0.0, goal, -1.0)
    goal = jnp.broadcast_to(jnp.concatenate([goal, goal], axis=0), (2 * NREP, LANES)).T[0:1, :]
    line = lax.broadcasted_iota(I32, (NREP * 32, 2 * NREP), 0)
    column = lax.broadcasted_iota(I32, (NREP * 32, 2 * NREP), 1)
    to = ((mx + line // 256) % NX) * NZ + (mz + (line // 32) % NZ) % NZ
    part = line % 32
    for_slot = (part < 16) & (goal == (to * SLOTS + ROWS + part // 2).astype(F32))
    for_own = (part >= 16) & (part < 18) & (column % NREP == to)
    wanted = (for_slot | for_own) & (column // NREP == part % 2)
    route[...] = jnp.where(wanted, 1.0, 0.0).astype(BF16)

    pltpu.make_async_copy(trec, trec, recv_sem.at[2]).wait()
    low = trec[0]
    for n in range(1, TP):
        low = low + trec[n]
    low = low.astype(BF16).astype(F32)
    other = pltpu.roll(low, RANK, 1)
    spread = jnp.concatenate(
        [jnp.where(lane32 < RANK, low, other), jnp.where(lane32 < RANK, other, low)], axis=0
    )
    both = jnp.concatenate([spread] * 2, axis=1)
    term = jnp.zeros((2 * NREP, LANES), F32)
    for g in range(4):
        lines = slice(g * 4 * RANK, (g + 1) * 4 * RANK)
        wide = jnp.where(chosen[:, lines], both, 0.0).astype(BF16)
        term = term + jnp.dot(wide, upv[lines, :], preferred_element_type=F32)
    term = term.astype(BF16)
    head = pl.ds(0, 18)
    for dx in (2, 1, 3, 0):
        lines = pl.ds(dx * NZ * 32, NZ * 32)
        routed = jnp.dot(route[lines], term, preferred_element_type=F32)
        sb3[dx * NZ : (dx + 1) * NZ] = routed.astype(BF16).reshape(NZ, 32, LANES)
        for dz in (4, 3, 5, 2, 6, 1, 7, 0):
            part_of = sb3.at[dx * NZ + dz, head]
            if dx or dz:
                pltpu.make_async_remote_copy(
                    part_of, mvrec.at[me, head], send_sem.at[3], recv_sem.at[3], device_id=(to_x[dx] + to_z[dz], tp),
                    device_id_type=MESH,
                ).start()
            else:
                pltpu.make_async_copy(part_of, mvrec.at[me, head], recv_sem.at[3]).start()

    received(grec, 34, 1)
    for n in range(ROWS):
        safe = jnp.clip(code_s[n], 0, 2 * NREP - 1)
        shift = (LANES - jnp.clip(line_s[n], 0, ROWS - 1) * 16) % LANES
        wq[2 * n : 2 * n + 2, :] = pltpu.roll(grec[safe // 2, 32:48].astype(F32), shift, 1)[0:2]
    column = wq[...].T[0:16, :] * 0.5
    for n in range(ROWS):
        safe = jnp.clip(code_s[n], 0, 2 * NREP - 1)
        one, two = grec[safe // 2, 0:16].astype(F32), grec[safe // 2, 16:32].astype(F32)
        base[n] = jnp.where(code_s[n] >= 0, jnp.where(safe % 2 == 1, two, one), 0.0)
        gain0[n] = jnp.broadcast_to(column[:, 2 * n : 2 * n + 1], (16, LANES))
        gain1[n] = jnp.broadcast_to(column[:, 2 * n + 1 : 2 * n + 2], (16, LANES))
    received(mvrec, 18, 3)
    for r in range(ROWS):
        back = mvrec[owners[r], 16:32].astype(F32)
        value0 = (pvs[r : r + 1, :] + 0.5 * back[0:1]).astype(BF16).astype(F32)
        value1 = (pvs[ROWS + r : ROWS + r + 1, :] + 0.5 * back[1:2]).astype(BF16).astype(F32)
        done = (mixed[r] + wn0s[r] * value0 + wn1s[r] * value1).astype(BF16)
        kept = slots[r] == me * SLOTS + r
        out[r] = jnp.where(kept, done, jnp.zeros((16, LANES), BF16))
    extra = mvrec[0, 0:16].astype(F32)
    for n in range(1, NREP):
        extra = extra + mvrec[n, 0:16].astype(F32)
    for n in range(ROWS):
        added = gain0[n] * extra[2 * n : 2 * n + 1] + gain1[n] * extra[2 * n + 1 : 2 * n + 2]
        out[ROWS + n] = (base[n] + added).astype(BF16)

    def sent(ref, n):
        pltpu.make_async_copy(ref, ref, send_sem.at[n]).wait()

    others = pl.ds(0, NREP - 1)
    sent(sb.at[others, pl.ds(0, 18)], 0)
    sent(mrec.at[others], 4)
    sent(sb4.at[others, pl.ds(0, 34)], 1)
    sent(trec.at[pl.ds(0, TP - 1)], 2)
    sent(sb3.at[others, pl.ds(0, 18)], 3)


def shards(hidden, queries, wk, wv, down, up, ridx, home, table, lengths, serve, kc, vc):
    hid = hidden.reshape(ROWS, 2, CHUNKS, LANES).transpose(0, 2, 1, 3).reshape(ROWS, LANES, LANES)
    qin = queries.reshape(ROWS, 2, 8, LANES).transpose(0, 2, 1, 3).reshape(ROWS, 16, LANES)
    dn = jnp.swapaxes(down, 1, 2)
    upr = up.reshape(ADP * RANK, LANES)
    vmem, smem = pltpu.VMEM, pltpu.SMEM
    scratch = [
        vmem((ROWS, LANES, LANES), BF16), vmem((ROWS, 16, LANES), BF16), vmem((8192, LANES), BF16), vmem((8192, LANES), BF16),
        vmem((ADP, RANK, 1024), BF16), vmem((ADP * RANK, LANES), BF16), vmem((64, LANES, LANES), BF16), vmem((64, LANES, LANES), BF16),
        smem((8,), I32), smem((512,), I32), smem((8, 8), I32), smem((1, 8), I32), smem((8,), I32),
        vmem((ROWS * LANES, LANES), F32), vmem((16, 8192), BF16),
        vmem((NREP, 32, LANES), BF16), vmem((NREP, 32, LANES), BF16),
        vmem((NREP * 16, LANES), F32), vmem((NREP * 16, LANES), F32), vmem((2 * NREP, 1024), BF16),
        vmem((1, LANES), I32), vmem((NREP, 1, LANES), I32),
        vmem((NREP, LANES), F32), vmem((TP, NREP, LANES), F32),
        vmem((ROWS, 16, LANES), F32), vmem((ROWS, 16, LANES), F32), vmem((ROWS, 16, LANES), F32),
        vmem((16, LANES), F32), vmem((16, LANES), F32),
        vmem((ROWS, 16, LANES), BF16), vmem((ROWS, 16, LANES), F32),
        vmem((NREP, 48, LANES), BF16), vmem((NREP, 48, LANES), BF16),
        vmem((NREP * 32, 2 * NREP), BF16), vmem((NREP, 32, LANES), BF16), vmem((NREP, 32, LANES), BF16),
        vmem((ROWS, 16, LANES), F32), vmem((ROWS, 16, LANES), F32), vmem((ROWS, 16, LANES), F32),
        vmem((8, LANES), I32), smem((8, LANES), I32), smem((ROWS,), I32), smem((ROWS,), I32), vmem((16, LANES), F32),
        pltpu.SemaphoreType.DMA((14,)), pltpu.SemaphoreType.DMA((5,)), pltpu.SemaphoreType.DMA((5,)),
    ]
    hid, qin, wk, wv, dn, upr, ridx, home, table, lengths, serve, kc, vc = (pltpu.with_memory_space_constraint(a, pltpu.HBM) for a in (hid, qin, wk, wv, dn, upr, ridx, home, table, lengths, serve, kc, vc))
    result = pl.pallas_call(
        kernel,
        out_shape=jax.ShapeDtypeStruct((SLOTS, 16, LANES), BF16),
        in_specs=[pl.BlockSpec(memory_space=pltpu.HBM)] * 13,
        out_specs=pl.BlockSpec(memory_space=pltpu.VMEM),
        scratch_shapes=scratch,
        compiler_params=pltpu.CompilerParams(
            collective_id=0, has_side_effects=True, vmem_limit_bytes=48 << 20
        ),
        name="decode",
    )(hid, qin, wk, wv, dn, upr, ridx, home, table, lengths, serve, kc, vc)
    return result.reshape(SLOTS, 8, 2, LANES).transpose(0, 2, 1, 3).reshape(SLOTS, 2, 1024)


def solution(mesh):
    placed = (
        P("rep", None, None),
        P("rep", None, "tp"),
        P(None, "tp"),
        P(None, "tp"),
        P("rep", "tp", None),
        P("rep", None, "tp"),
        P("rep"),
        P(),
        P("rep", None),
        P("rep", None),
        P("rep"),
        P("rep", None, "tp"),
        P("rep", None, "tp"),
    )
    return jax.shard_map(
        shards, mesh=mesh, in_specs=placed, out_specs=P("rep", None, "tp"), check_vma=False
    )
```
